32 devices in a mesh: dom: 8 (over z, y), col: 4 (over x, core).
Axes of the slice: x: 2, y: 2, z: 4, core: 2. Of those that a mesh axis runs over, the one named last changes fastest.
Arguments:
- right_side: float32 [3, 64, 32768], P(None, 'col', 'dom'), may hold values from -90 to 90, as said below
- stiffness: float32 [64, 32768], P(None, 'dom'), may hold values from -1 to 9, as said below
- contact: float32 [64, 32768], P(None, 'dom'), may hold values from -1 to 60, as said below
- pair_local: int32 [512], P('dom'), may hold values from 0 to 63
- pair_partner: int32 [512], P('dom'), may hold values from 0 to 71, as said below
- pair_count: int32 [8], P('dom'), may hold values from 16 to 64, as said below
- objective_weight: float32 [3, 32768], P(None, 'dom'), may hold values from -20 to 20
Outputs:
- solution_field: float32 [3, 64, 32768], P(None, 'col', 'dom')
- residual: float32 [3, 64, 32768], P(None, 'col', 'dom')
- param_step: float32 [64], P('col')
The draws below stay inside these ranges and needn't reach their ends.
Inputs may be any that keep to these rules, and one draw needn't show every extreme that they name: `right_side`: varies from node to node. `stiffness`: every patch's block is symmetric and diagonally dominant with a positive diagonal. `contact`: every slot's block is symmetric and diagonally dominant with a nonnegative diagonal. `pair_partner`: A value below 64 names another patch of the slot's own partition; a value 64 + q names patch q of the next partition, with q below 8; slots of the last partition name only their own partition. `pair_count`: some partition has all 64 slots live.
All inputs are finite; a program needn't handle non-finite values.
Results may differ from the reference program's by a relative error of at most 0.0003.
Values sent between devices are 32-bit elements; how exact they have to be, the bound alone decides.
No kernel may reach another device: no remote copies, remote signals or barrier semaphores. Data moves between devices by JAX's collectives and lax.ppermute only.
A program may use at most 64 MiB of HBM per device.

```python
import math
import jax
import jax.numpy as jnp
from jax import lax

PN = 64
P_DEV = 64
NB = 8
COLS = 64
ITERS = 2
PATCHES = 512
PAIRS = 512
NODES = 32768
N_DOM = 8


def dominant_blocks(key, count, lo, hi):
    key_off, key_diag = jax.random.split(key, 2)
    raw = jax.random.uniform(key_off, (count, PN, PN), jnp.float32, -1.0, 1.0) / PN
    symmetric = (raw + jnp.transpose(raw, (0, 2, 1))) * 0.5
    identity = jnp.eye(PN, dtype=jnp.float32)
    extra = jnp.exp(jax.random.uniform(key_diag, (count, PN), jnp.float32, math.log(lo), math.log(hi)))
    blocks = symmetric * (1.0 - identity) + identity * (1.0 + extra[:, :, None])
    return blocks


def draw_stiffness(key, part):
    blocks = dominant_blocks(key, PATCHES, 0.1, 3.0)
    return jnp.transpose(blocks, (1, 0, 2)).reshape(PN, PATCHES * PN)


def draw_contact(key, part):
    key_block, key_scale = jax.random.split(jax.random.fold_in(key, 3), 2)
    blocks = dominant_blocks(key_block, PAIRS, 0.1, 3.0)
    strength = jnp.exp(jax.random.uniform(key_scale, (PAIRS,), jnp.float32, math.log(0.5), math.log(4.0)))
    blocks = blocks * strength[:, None, None]
    return jnp.transpose(blocks, (1, 0, 2)).reshape(PN, PAIRS * PN)


def pair_tables(key):
    key_one, key_two, key_three, key_four = jax.random.split(jax.random.fold_in(key, 11), 4)
    slot_index = jnp.arange(PAIRS, dtype=jnp.int32)
    owner_index = slot_index // P_DEV
    local_patch = jax.random.randint(key_one, (PAIRS,), 0, P_DEV, dtype=jnp.int32)
    local_patch = jnp.where(slot_index == 1, P_DEV - 1, local_patch)
    crossing = jax.random.randint(key_two, (PAIRS,), 0, 2, dtype=jnp.int32) * (owner_index < N_DOM - 1).astype(jnp.int32)
    own_partner = (local_patch + 1 + jax.random.randint(key_three, (PAIRS,), 0, P_DEV - 1, dtype=jnp.int32)) % P_DEV
    far_partner = P_DEV + jax.random.randint(key_four, (PAIRS,), 0, NB, dtype=jnp.int32)
    partner = jnp.where(crossing == 1, far_partner, own_partner)
    partner = jnp.where(slot_index == 0, P_DEV + NB - 1, partner)
    return (local_patch, partner)


def draw_pair_local(key, part):
    return pair_tables(key)[0]


def draw_pair_partner(key, part):
    return pair_tables(key)[1]


def draw_pair_count(key, part):
    key_one, key_two = jax.random.split(jax.random.fold_in(key, 17), 2)
    counts = jax.random.randint(key_one, (N_DOM,), max(2, P_DEV // 4), P_DEV + 1, dtype=jnp.int32)
    fullest = jax.random.randint(key_two, (), 0, N_DOM, dtype=jnp.int32)
    return jnp.where(jnp.arange(N_DOM, dtype=jnp.int32) == fullest, P_DEV, counts)


def draw_right_side(key, part):
    key_base, key_rough = jax.random.split(jax.random.fold_in(key, 23), 2)
    position = jnp.arange(NODES, dtype=jnp.float32) / (NODES - 1)
    trend = 1.0 + 2.0 * position
    rough = jnp.exp(math.log(10.0) * jax.random.uniform(key_rough, (NODES,), jnp.float32))
    column_scale = 1.0 + 2.0 * jnp.arange(COLS, dtype=jnp.float32) / (COLS - 1)
    base = jax.random.truncated_normal(key_base, -4.0, 4.0, (3, COLS, NODES), jnp.float32)
    return 0.25 * base * trend[None, None, :] * rough[None, None, :] * column_scale[None, :, None]


def draw_objective_weight(key, part):
    key_base = jax.random.fold_in(key, 29)
    position = jnp.arange(NODES, dtype=jnp.float32) / (NODES - 1)
    trend = 1.0 + 2.0 * position
    base = jax.random.truncated_normal(key_base, -4.0, 4.0, (3, NODES), jnp.float32)
    return base * trend[None, :]


def setup_inputs(seed: int = 0) -> dict:
    splits = jax.random.split(jax.random.key(seed), 8)
    return {
        "right_side": draw_right_side(jax.random.fold_in(splits[7], 71), 0),
        "stiffness": draw_stiffness(jax.random.fold_in(splits[7], 71), 0),
        "contact": draw_contact(jax.random.fold_in(splits[7], 71), 0),
        "pair_local": draw_pair_local(jax.random.fold_in(splits[7], 71), 0),
        "pair_partner": draw_pair_partner(jax.random.fold_in(splits[7], 71), 0),
        "pair_count": draw_pair_count(jax.random.fold_in(splits[7], 71), 0),
        "objective_weight": draw_objective_weight(jax.random.fold_in(splits[7], 71), 0),
    }


def operate(field, stiffness, contact, pair_local, pair_partner, pair_count):
    stiff_blocks = stiffness.reshape(PN, PATCHES, PN)
    pair_blocks = contact.reshape(PN, PAIRS, PN)
    pair_index = jnp.arange(PAIRS, dtype=jnp.int32)
    owner_index = pair_index // P_DEV
    first_patch = owner_index * P_DEV + pair_local
    second_patch = owner_index * P_DEV + pair_partner
    live_mask = (pair_index % P_DEV < pair_count[owner_index]).astype(jnp.float32)
    field_rows = field.reshape(3, COLS, PATCHES, PN)

    def apply_part(part_rows):
        elastic = jnp.einsum('cpi,ipj->cpj', part_rows, stiff_blocks, precision=lax.Precision.HIGHEST)
        gap_rows = (jnp.take(part_rows, first_patch, axis=1) - jnp.take(part_rows, second_patch, axis=1)) * live_mask[None, :, None]
        forces = jnp.einsum('cki,ikj->ckj', gap_rows, pair_blocks, precision=lax.Precision.HIGHEST)
        return elastic.at[:, first_patch].add(forces).at[:, second_patch].add(-forces)
    applied = lax.map(apply_part, field_rows)
    return applied.reshape(3, COLS, NODES)

def column_sums(left, right):
    return lax.optimization_barrier(jnp.sum(left * right, axis=(0, 2)))

def reference(right_side, stiffness, contact, pair_local, pair_partner, pair_count, objective_weight):
    solution_field = jnp.zeros_like(right_side)
    residual = right_side
    direction = right_side
    norm_now = column_sums(residual, residual)
    for iteration in range(ITERS):
        applied = operate(direction, stiffness, contact, pair_local, pair_partner, pair_count)
        step_size = norm_now / column_sums(direction, applied)
        solution_field = solution_field + step_size[None, :, None] * direction
        residual = residual - step_size[None, :, None] * applied
        norm_next = column_sums(residual, residual)
        direction = residual + (norm_next / norm_now)[None, :, None] * direction
        norm_now = norm_next
    gradient = lax.optimization_barrier(jnp.sum(objective_weight[:, None, :] * solution_field, axis=(0, 2)))
    param_step = gradient / jnp.sqrt(jnp.mean(gradient * gradient) + 1e-06)
    return (solution_field, residual, param_step)
```

```python
import functools

import jax
import jax.numpy as jnp
from jax import lax
from jax.experimental import pallas as pl
from jax.experimental.pallas import tpu as pltpu
from jax.sharding import PartitionSpec as P

PN = 64
NB = 8
LANES = 128
MOMENT_LANES = 256
VMEM = pl.BlockSpec(memory_space=pltpu.VMEM)
SMEM = pl.BlockSpec(memory_space=pltpu.SMEM)


def shifted(value, axis, by):
    count = lax.axis_size(axis)
    pairs = [(i, i + by) for i in range(count) if 0 <= i + by < count]
    return lax.ppermute(value, axis, pairs)


def left_half(shape):
    return lax.broadcasted_iota(jnp.int32, shape, len(shape) - 1) < PN


def split(value):
    high = value.astype(jnp.bfloat16)
    low = (value - high.astype(jnp.float32)).astype(jnp.bfloat16)
    return high, low


def tile(ref, index):
    return ref[:, index * LANES : (index + 1) * LANES]


def pair_product(rows, blocks):
    mask = left_half((PN, LANES)).astype(jnp.bfloat16)
    other = (1 - left_half((PN, LANES)).astype(jnp.int32)).astype(jnp.bfloat16)
    block_high, block_low = split(blocks)
    right_high = jnp.concatenate([block_high * mask, block_high * other], axis=0)
    right_low = jnp.concatenate([block_low * mask, block_low * other], axis=0)
    row_high, row_low = split(rows)
    dot = functools.partial(jnp.dot, preferred_element_type=jnp.float32)
    return dot(row_high, right_high) + (dot(row_low, right_high) + dot(row_high, right_low))


def fill_twins(field_tile, twin_ref, patch):
    swapped = pltpu.roll(field_tile, PN, 1)
    left = left_half(field_tile.shape)
    twin_ref[patch] = jnp.where(left, field_tile, swapped)
    twin_ref[patch + 1] = jnp.where(left, swapped, field_tile)


def elastic(field_tile, blocks, total_ref, patch):
    product = pair_product(field_tile, blocks)
    left = left_half(product.shape)
    total_ref[patch] = jnp.where(left, product, 0.0)
    total_ref[patch + 1] = jnp.where(left, 0.0, product)


def contacts(twin_ref, contact_ref, local_ref, partner_ref, count_ref, total_ref):
    rows = twin_ref.shape[1]
    left = left_half((rows, LANES))
    live_count = count_ref[0]
    for step in range(contact_ref.shape[1] // LANES):
        slot = 2 * step
        first_a, first_b = local_ref[slot], partner_ref[slot]
        second_a, second_b = local_ref[slot + 1], partner_ref[slot + 1]
        first_live = jnp.where(slot < live_count, 1.0, 0.0)
        second_live = jnp.where(slot + 1 < live_count, 1.0, 0.0)
        first_gap = (twin_ref[first_a] - twin_ref[first_b]) * first_live
        second_gap = (twin_ref[second_a] - twin_ref[second_b]) * second_live
        force = pair_product(jnp.where(left, first_gap, second_gap), tile(contact_ref, step))
        first_force = jnp.where(left, force, 0.0)
        second_force = jnp.where(left, 0.0, force)
        total_ref[first_a] = total_ref[first_a] + first_force
        total_ref[first_b] = total_ref[first_b] - first_force
        total_ref[second_a] = total_ref[second_a] + second_force
        total_ref[second_b] = total_ref[second_b] - second_force


def folded(total_ref, patch):
    first, second = total_ref[patch], total_ref[patch + 1]
    first = first + pltpu.roll(first, PN, 1)
    second = second + pltpu.roll(second, PN, 1)
    return jnp.where(left_half(first.shape), first, second)


def clear(total_ref, start, stop):
    zero = jnp.zeros(total_ref.shape[1:], jnp.float32)
    for patch in range(start, stop):
        total_ref[patch] = zero


def first_kernel(
    local_ref, partner_ref, count_ref, field_ref, halo_ref, stiff_ref, contact_ref,
    image_ref, lead_ref, spread_ref, twin_ref, total_ref,
):
    patches = field_ref.shape[1] // PN
    for index in range(patches // 2):
        field_tile = tile(field_ref, index)
        fill_twins(field_tile, twin_ref, 2 * index)
        elastic(field_tile, tile(stiff_ref, index), total_ref, 2 * index)
    for index in range(NB // 2):
        fill_twins(tile(halo_ref, index), twin_ref, patches + 2 * index)
    clear(total_ref, patches, patches + NB)
    contacts(twin_ref, contact_ref, local_ref, partner_ref, count_ref, total_ref)
    for index in range(patches // 2):
        value = folded(total_ref, 2 * index)
        image_ref[:, index * LANES : (index + 1) * LANES] = value
        if index < NB // 2:
            lead_ref[:, index * LANES : (index + 1) * LANES] = value
    for index in range(NB // 2):
        spread_ref[:, index * LANES : (index + 1) * LANES] = folded(total_ref, patches + 2 * index)


def by_column(product, columns):
    total = product[:columns]
    for part in range(1, product.shape[0] // columns):
        total = total + product[part * columns : (part + 1) * columns]
    return total


def second_kernel(
    local_ref, partner_ref, count_ref, field_ref, halo_ref, image_ref, spread_ref, received_ref, far_ref,
    stiff_ref, contact_ref, weight_ref,
    twice_ref, moment_ref, far_spread_ref, twin_ref, total_ref, *, columns,
):
    rows = field_ref.shape[0]
    patches = field_ref.shape[1] // PN
    tiles = patches // 2
    lead = NB // 2
    across = jnp.zeros((columns, LANES), jnp.float32)
    square = jnp.zeros((columns, LANES), jnp.float32)
    for index in range(tiles):
        image_tile = tile(image_ref, index)
        if index < lead:
            image_tile = image_tile + tile(received_ref, index)
        fill_twins(image_tile, twin_ref, 2 * index)
        elastic(image_tile, tile(stiff_ref, index), total_ref, 2 * index)
        across = across + by_column(tile(field_ref, index) * image_tile, columns)
        square = square + by_column(image_tile * image_tile, columns)
    across = jnp.sum(across, axis=1, keepdims=True)
    square = jnp.sum(square, axis=1, keepdims=True)
    trial = jnp.where(square > 0.0, across / jnp.where(square > 0.0, square, 1.0), 0.0)
    trial = jnp.broadcast_to(trial, (columns, LANES))
    trial_rows = jnp.concatenate([trial] * (rows // columns), axis=0)
    for index in range(lead):
        far_tile = tile(far_ref, index) + tile(spread_ref, index)
        fill_twins(far_tile, twin_ref, patches + 2 * index)
    clear(total_ref, patches, patches + NB)
    contacts(twin_ref, contact_ref, local_ref, partner_ref, count_ref, total_ref)
    sums = [jnp.zeros((columns, LANES), jnp.float32) for _ in range(12)]

    def add(place, product):
        sums[place] = sums[place] + by_column(product, columns)

    for index in range(tiles):
        field_tile = tile(field_ref, index)
        image_tile = tile(image_ref, index)
        if index < lead:
            image_tile = image_tile + tile(received_ref, index)
        twice_tile = folded(total_ref, 2 * index)
        twice_ref[:, index * LANES : (index + 1) * LANES] = twice_tile
        rest = field_tile - trial_rows * image_tile
        image_rest = image_tile - trial_rows * twice_tile
        weight_tile = jnp.concatenate(
            [
                jnp.broadcast_to(weight_ref[part : part + 1, index * LANES : (index + 1) * LANES], (columns, LANES))
                for part in range(rows // columns)
            ],
            axis=0,
        )
        add(0, field_tile * field_tile)
        add(1, field_tile * image_tile)
        add(2, rest * rest)
        add(3, rest * image_tile)
        add(4, image_tile * image_tile)
        add(5, rest * image_rest)
        add(6, rest * twice_tile + image_tile * image_rest)
        add(7, image_tile * twice_tile)
        add(10, weight_tile * field_tile)
        add(11, weight_tile * image_tile)
    for index in range(lead):
        far_spread = folded(total_ref, patches + 2 * index)
        far_spread_ref[:, index * LANES : (index + 1) * LANES] = far_spread
        far_tile = tile(far_ref, index) + tile(spread_ref, index)
        add(8, (tile(halo_ref, index) - trial_rows * far_tile) * far_spread)
        add(9, far_tile * far_spread)
    lane = lax.broadcasted_iota(jnp.int32, (columns, LANES), 1)
    table = jnp.where(lane == 12, trial, 0.0)
    for place in range(12):
        table = jnp.where(lane == place, jnp.sum(sums[place], axis=1, keepdims=True), table)
    table = jnp.concatenate([table, jnp.zeros((LANES - columns, LANES), jnp.float32)], axis=0)
    flipped = jnp.transpose(table)
    for half in range(2):
        part = flipped[half * 8 : half * 8 + 8]
        row = pltpu.roll(part, 0, 1, stride=columns, stride_axis=0)
        row = jnp.sum(row, axis=0, keepdims=True)
        moment_ref[:, half * LANES : (half + 1) * LANES] = jnp.broadcast_to(row, (moment_ref.shape[0], LANES))


def last_kernel(
    place_ref, moment_ref, field_ref, image_ref, received_ref, twice_ref, far_received_ref,
    solution_ref, residual_ref, step_ref, *, columns, groups,
):
    rows = field_ref.shape[0]
    devices = moment_ref.shape[0]

    def moment(place):
        half = place // 8
        value = moment_ref[:, half * LANES : (half + 1) * LANES]
        shift = (LANES - columns * (place % 8)) % LANES
        if shift:
            value = pltpu.roll(value, shift, 1)
        return value.reshape(devices // 8, 8, LANES)

    def total(value):
        value = jnp.sum(value, axis=0)
        width = groups
        while width < 8:
            value = value + pltpu.roll(value, width, 0)
            width *= 2
        return value

    norm = total(moment(0))
    bend = total(moment(1))
    first_step = norm / bend
    change = first_step[None] - moment(12)
    square = moment(4)
    mixed = moment(3)
    norm_next = total(moment(2) - 2.0 * change * mixed + change * change * square)
    drift = total(mixed - change * square)
    curve = total(
        moment(5) - change * moment(6) + change * change * moment(7)
        - first_step[None] * (moment(8) - change * moment(9))
    )
    ratio = norm_next / norm
    bend_next = curve + 2.0 * ratio * drift + ratio * ratio * bend
    second_step = norm_next / bend_next
    on_field = first_step + second_step * (1.0 + ratio)
    on_image = -second_step * first_step
    gradient = on_field * total(moment(10)) + on_image * total(moment(11))
    lane = lax.broadcasted_iota(jnp.int32, (8, LANES), 1)
    row = lax.broadcasted_iota(jnp.int32, (8, LANES), 0)
    counted = jnp.where((lane < columns) & (row < groups), gradient * gradient, 0.0)
    square_total = jnp.sum(jnp.sum(counted, axis=1, keepdims=True), axis=0, keepdims=True)
    scaled = gradient / jnp.sqrt(square_total / (columns * groups) + 1e-06)
    mine = row == place_ref[0]

    def own(value):
        return jnp.sum(jnp.where(mine, value, 0.0), axis=0, keepdims=True)

    step_ref[...] = own(scaled)[:, :columns]
    pair = jnp.concatenate([own(on_field), own(on_image), jnp.zeros((LANES - 2, LANES), jnp.float32)], axis=0)
    flipped = jnp.transpose(pair)[:columns]
    field_rows = jnp.concatenate([jnp.broadcast_to(flipped[:, 0:1], (columns, LANES))] * (rows // columns), axis=0)
    image_rows = jnp.concatenate([jnp.broadcast_to(flipped[:, 1:2], (columns, LANES))] * (rows // columns), axis=0)
    for index in range(field_ref.shape[1] // LANES):
        field_tile = tile(field_ref, index)
        image_tile = tile(image_ref, index)
        twice_tile = tile(twice_ref, index)
        if index < NB // 2:
            image_tile = image_tile + tile(received_ref, index)
            twice_tile = twice_tile + tile(far_received_ref, index)
        where = slice(index * LANES, (index + 1) * LANES)
        solution_ref[:, where] = field_rows * field_tile + image_rows * image_tile
        residual_ref[:, where] = field_tile - field_rows * image_tile - image_rows * twice_tile


def shards(right_side, stiffness, contact, pair_local, pair_partner, pair_count, objective_weight):
    components, columns, nodes = right_side.shape
    rows = components * columns
    patches = nodes // PN
    groups = lax.axis_size("col")
    devices = lax.axis_size("dom") * groups
    f32 = jnp.float32
    field = right_side.reshape(rows, nodes)
    width = NB * PN
    halo = shifted(right_side[:, :, :width], "dom", -1).reshape(rows, width)
    params = pltpu.CompilerParams(vmem_limit_bytes=48 * 1024 * 1024)
    scratch = [pltpu.VMEM((patches + NB, rows, LANES), f32)] * 2
    wide = jax.ShapeDtypeStruct((rows, nodes), f32)
    narrow = jax.ShapeDtypeStruct((rows, width), f32)
    image, lead, spread = pl.pallas_call(
        first_kernel,
        out_shape=(wide, narrow, narrow),
        in_specs=[SMEM] * 3 + [VMEM] * 4,
        out_specs=(VMEM,) * 3,
        scratch_shapes=scratch,
        compiler_params=params,
        name="first",
    )(pair_local, pair_partner, pair_count, field, halo, stiffness, contact)
    far = shifted(lead, "dom", -1)
    received = shifted(spread, "dom", 1)
    twice, moments, far_spread = pl.pallas_call(
        functools.partial(second_kernel, columns=columns),
        out_shape=(wide, jax.ShapeDtypeStruct((devices, MOMENT_LANES), f32), narrow),
        in_specs=[SMEM] * 3 + [VMEM] * 9,
        out_specs=(VMEM,) * 3,
        scratch_shapes=scratch,
        compiler_params=params,
        name="second",
    )(
        pair_local, pair_partner, pair_count, field, halo, image, spread, received, far,
        stiffness, contact, objective_weight,
    )
    far_received = shifted(far_spread, "dom", 1)
    gathered = lax.all_to_all(moments, ("dom", "col"), 0, 0, tiled=True)
    place = lax.axis_index("col").astype(jnp.int32).reshape(1)
    solution_field, residual, step = pl.pallas_call(
        functools.partial(last_kernel, columns=columns, groups=groups),
        out_shape=(wide, wide, jax.ShapeDtypeStruct((1, columns), f32)),
        in_specs=[SMEM] + [VMEM] * 6,
        out_specs=(VMEM,) * 3,
        compiler_params=params,
        name="last",
    )(place, gathered, field, image, received, twice, far_received)
    return (
        solution_field.reshape(right_side.shape),
        residual.reshape(right_side.shape),
        step.reshape(columns),
    )


def solution(mesh):
    placed = (
        P(None, "col", "dom"),
        P(None, "dom"),
        P(None, "dom"),
        P("dom"),
        P("dom"),
        P("dom"),
        P(None, "dom"),
    )
    return jax.shard_map(
        shards,
        mesh=mesh,
        in_specs=placed,
        out_specs=(P(None, "col", "dom"), P(None, "col", "dom"), P("col")),
        check_vma=False,
    )
```

```python
import functools

import jax
import jax.numpy as jnp
from jax import lax
from jax.experimental import pallas as pl
from jax.experimental.pallas import tpu as pltpu
from jax.sharding import PartitionSpec as P

PN = 64
NB = 8
LANES = 128
MOMENT_LANES = 256
VMEM = pl.BlockSpec(memory_space=pltpu.VMEM)
SMEM = pl.BlockSpec(memory_space=pltpu.SMEM)
HBM = pl.BlockSpec(memory_space=pltpu.HBM)
SUMS = 12


def shifted(value, axis, by):
    count = lax.axis_size(axis)
    pairs = [(i, i + by) for i in range(count) if 0 <= i + by < count]
    return lax.ppermute(value, axis, pairs)


def swapped(value, axis, odd):
    count = lax.axis_size(axis)
    pairs = []
    for low in range(1 if odd else 0, count, 2):
        high = (low + 1) % count
        pairs += [(low, high), (high, low)]
    return lax.ppermute(value, axis, pairs)


def left_half(shape):
    return lax.broadcasted_iota(jnp.int32, shape, len(shape) - 1) < PN


def split(value):
    high = value.astype(jnp.bfloat16)
    low = (value - high.astype(jnp.float32)).astype(jnp.bfloat16)
    return high, low


def tile(ref, index):
    return ref[:, index * LANES : (index + 1) * LANES]


def put(ref, index, value):
    ref[:, index * LANES : (index + 1) * LANES] = value


def block_diagonal(high, low):
    mask = left_half((PN, LANES)).astype(jnp.bfloat16)
    other = (1 - left_half((PN, LANES)).astype(jnp.int32)).astype(jnp.bfloat16)
    return (
        jnp.concatenate([high * mask, high * other], axis=0),
        jnp.concatenate([low * mask, low * other], axis=0),
    )


def pair_product(rows, high, low):
    right_high, right_low = block_diagonal(high, low)
    row_high, row_low = split(rows)
    dot = functools.partial(jnp.dot, preferred_element_type=jnp.float32)
    return dot(row_high, right_high) + (dot(row_low, right_high) + dot(row_high, right_low))


def fill_twins(field_tile, twin_ref, patch):
    swapped = pltpu.roll(field_tile, PN, 1)
    left = left_half(field_tile.shape)
    twin_ref[patch] = jnp.where(left, field_tile, swapped)
    twin_ref[patch + 1] = jnp.where(left, swapped, field_tile)


def contacts(twin_ref, high_ref, low_ref, local_ref, partner_ref, count_ref, total_ref):
    rows = twin_ref.shape[1]
    left = left_half((rows, LANES))
    live_count = count_ref[0]
    for step in range(high_ref.shape[1] // LANES):
        slot = 2 * step
        first_a, first_b = local_ref[slot], partner_ref[slot]
        second_a, second_b = local_ref[slot + 1], partner_ref[slot + 1]
        first_live = jnp.where(slot < live_count, 1.0, 0.0)
        second_live = jnp.where(slot + 1 < live_count, 1.0, 0.0)
        first_gap = (twin_ref[first_a] - twin_ref[first_b]) * first_live
        second_gap = (twin_ref[second_a] - twin_ref[second_b]) * second_live
        force = pair_product(
            jnp.where(left, first_gap, second_gap), tile(high_ref, step), tile(low_ref, step)
        )
        first_force = jnp.where(left, force, 0.0)
        second_force = jnp.where(left, 0.0, force)
        total_ref[first_a] = total_ref[first_a] + first_force
        total_ref[first_b] = total_ref[first_b] - first_force
        total_ref[second_a] = total_ref[second_a] + second_force
        total_ref[second_b] = total_ref[second_b] - second_force


def folded(total_ref, patch):
    first, second = total_ref[patch], total_ref[patch + 1]
    first = first + pltpu.roll(first, PN, 1)
    second = second + pltpu.roll(second, PN, 1)
    return jnp.where(left_half(first.shape), first, second)


def clear(total_ref):
    zero = jnp.zeros(total_ref.shape[1:], jnp.float32)
    for patch in range(total_ref.shape[0]):
        total_ref[patch] = zero


def prepare_kernel(
    field_hbm, stiff_hbm, contact_hbm,
    field_ref, elastic_ref, stiff_high_ref, stiff_low_ref, contact_high_ref, contact_low_ref,
    stiff_ref, contact_ref, sems,
):
    patches = field_ref.shape[1] // PN
    copies = [
        pltpu.make_async_copy(field_hbm, field_ref, sems.at[0]),
        pltpu.make_async_copy(stiff_hbm, stiff_ref, sems.at[1]),
        pltpu.make_async_copy(contact_hbm, contact_ref, sems.at[2]),
    ]
    for copy in copies:
        copy.start()
    copies[0].wait()
    copies[1].wait()
    for index in range(patches // 2):
        field_tile = tile(field_ref, index)
        high, low = split(tile(stiff_ref, index))
        put(stiff_high_ref, index, high)
        put(stiff_low_ref, index, low)
        put(elastic_ref, index, pair_product(field_tile, high, low))
    copies[2].wait()
    for index in range(contact_ref.shape[1] // LANES):
        high, low = split(tile(contact_ref, index))
        put(contact_high_ref, index, high)
        put(contact_low_ref, index, low)


def couple_kernel(
    local_ref, partner_ref, count_ref, chain_ref, field_ref, elastic_ref, halo_ref, high_ref, low_ref,
    image_ref, spread_ref, even_ref, odd_ref, twin_ref, total_ref,
):
    patches = image_ref.shape[1] // PN
    lead = NB // 2
    clear(total_ref)
    for index in range(patches // 2):
        fill_twins(tile(field_ref, index), twin_ref, 2 * index)
    for index in range(lead):
        fill_twins(tile(halo_ref, index), twin_ref, patches + 2 * index)
    contacts(twin_ref, high_ref, low_ref, local_ref, partner_ref, count_ref, total_ref)
    even = chain_ref[0] % 2 == 0
    for index in range(patches // 2):
        value = tile(elastic_ref, index) + folded(total_ref, 2 * index)
        put(image_ref, index, value)
        if index < lead:
            spread = folded(total_ref, patches + 2 * index)
            put(spread_ref, index, spread)
            put(even_ref, index, jnp.where(even, spread, value))
            put(odd_ref, index, jnp.where(even, value, spread))


def by_column(product, columns):
    total = product[:columns]
    for part in range(1, product.shape[0] // columns):
        total = total + product[part * columns : (part + 1) * columns]
    return total


class Sums:
    def __init__(self, columns):
        self.columns = columns
        self.values = {}

    def add(self, place, product):
        product = by_column(product, self.columns)
        self.values[place] = self.values[place] + product if place in self.values else product

    def load(self, ref):
        for place in range(SUMS):
            self.values[place] = ref[place * self.columns : (place + 1) * self.columns]

    def store(self, ref):
        for place in range(SUMS):
            zero = jnp.zeros((self.columns, LANES), jnp.float32)
            ref[place * self.columns : (place + 1) * self.columns] = self.values.get(place, zero)


def weights_of(weight_ref, index, rows):
    parts = weight_ref.shape[0]
    return jnp.concatenate(
        [
            jnp.broadcast_to(weight_ref[part : part + 1, index * LANES : (index + 1) * LANES], (rows // parts, LANES))
            for part in range(parts)
        ],
        axis=0,
    )


def lift_kernel(
    field_ref, image_ref, stiff_high_ref, stiff_low_ref, weight_ref,
    elastic_ref, sums_ref, trial_ref, *, columns,
):
    rows = field_ref.shape[0]
    patches = field_ref.shape[1] // PN
    lead = NB // 2
    sums = Sums(columns)
    for index in range(patches // 2):
        field_tile = tile(field_ref, index)
        weight_tile = weights_of(weight_ref, index, rows)
        sums.add(0, field_tile * field_tile)
        sums.add(10, weight_tile * field_tile)
        if index < lead:
            continue
        image_tile = tile(image_ref, index)
        product = pair_product(image_tile, tile(stiff_high_ref, index), tile(stiff_low_ref, index))
        put(elastic_ref, index - lead, product)
        sums.add(1, field_tile * image_tile)
        sums.add(4, image_tile * image_tile)
        sums.add(11, weight_tile * image_tile)
    across = jnp.sum(sums.values[1], axis=1, keepdims=True)
    square = jnp.sum(sums.values[4], axis=1, keepdims=True)
    some = square > 0.0
    trial = jnp.where(some, across / jnp.where(some, square, 1.0), 0.0)
    trial = jnp.broadcast_to(trial, (columns, LANES))
    trial_ref[...] = trial
    trial_rows = jnp.concatenate([trial] * (rows // columns), axis=0)
    for index in range(lead, patches // 2):
        image_tile = tile(image_ref, index)
        rest = tile(field_ref, index) - trial_rows * image_tile
        sums.add(2, rest * rest)
        sums.add(3, rest * image_tile)
    sums.store(sums_ref)


def second_kernel(
    local_ref, partner_ref, count_ref, chain_ref, field_ref, halo_ref, image_ref, spread_ref, even_ref, odd_ref,
    stiff_high_ref, stiff_low_ref, contact_high_ref, contact_low_ref, weight_ref, sums_ref, trial_ref, elastic_ref,
    twice_ref, lead_ref, moment_ref, far_spread_ref, twin_ref, total_ref, *, columns,
):
    rows = field_ref.shape[0]
    patches = field_ref.shape[1] // PN
    lead = NB // 2
    place, last = chain_ref[0], chain_ref[1] - 1
    even = place % 2 == 0
    trial = trial_ref[...]
    trial_rows = jnp.concatenate([trial] * (rows // columns), axis=0)
    sums = Sums(columns)
    sums.load(sums_ref)
    far_tiles = []
    products = []
    clear(total_ref)
    for index in range(lead, patches // 2):
        fill_twins(tile(image_ref, index), twin_ref, 2 * index)
    for index in range(lead):
        first, second = tile(even_ref, index), tile(odd_ref, index)
        received = jnp.where(place > 0, jnp.where(even, second, first), 0.0)
        far_tile = jnp.where(place < last, jnp.where(even, first, second) + tile(spread_ref, index), 0.0)
        far_tiles.append(far_tile)
        fill_twins(far_tile, twin_ref, patches + 2 * index)
        field_tile = tile(field_ref, index)
        image_tile = tile(image_ref, index) + received
        put(lead_ref, index, image_tile)
        fill_twins(image_tile, twin_ref, 2 * index)
        products.append(pair_product(image_tile, tile(stiff_high_ref, index), tile(stiff_low_ref, index)))
        rest = field_tile - trial_rows * image_tile
        sums.add(1, field_tile * image_tile)
        sums.add(2, rest * rest)
        sums.add(3, rest * image_tile)
        sums.add(4, image_tile * image_tile)
        sums.add(11, weights_of(weight_ref, index, rows) * image_tile)
    contacts(twin_ref, contact_high_ref, contact_low_ref, local_ref, partner_ref, count_ref, total_ref)
    for index in range(patches // 2):
        image_tile = tile(lead_ref if index < lead else image_ref, index)
        product = products[index] if index < lead else tile(elastic_ref, index - lead)
        twice_tile = product + folded(total_ref, 2 * index)
        put(twice_ref, index, twice_tile)
        rest = tile(field_ref, index) - trial_rows * image_tile
        image_rest = image_tile - trial_rows * twice_tile
        sums.add(5, rest * image_rest)
        sums.add(6, rest * twice_tile + image_tile * image_rest)
        sums.add(7, image_tile * twice_tile)
    for index in range(lead):
        far_spread = folded(total_ref, patches + 2 * index)
        put(far_spread_ref, index, far_spread)
        sums.add(8, (tile(halo_ref, index) - trial_rows * far_tiles[index]) * far_spread)
        sums.add(9, far_tiles[index] * far_spread)
    lane = lax.broadcasted_iota(jnp.int32, (columns, LANES), 1)
    table = jnp.where(lane == SUMS, trial, 0.0)
    for number in range(SUMS):
        table = jnp.where(lane == number, jnp.sum(sums.values[number], axis=1, keepdims=True), table)
    table = jnp.concatenate([table, jnp.zeros((LANES - columns, LANES), jnp.float32)], axis=0)
    flipped = jnp.transpose(table)
    for half in range(2):
        row = pltpu.roll(flipped[half * 8 : half * 8 + 8], 0, 1, stride=columns, stride_axis=0)
        row = jnp.sum(row, axis=0, keepdims=True)
        moment_ref[:, :, half * LANES : (half + 1) * LANES] = jnp.broadcast_to(
            row[None], (moment_ref.shape[0], 1, LANES)
        )


def relay_kernel(value_ref, out_ref):
    out_ref[...] = value_ref[...]


def last_kernel(
    place_ref, moment_ref, field_ref, image_ref, lead_ref, twice_ref, far_received_ref,
    solution_ref, residual_ref, step_ref, *, columns, groups,
):
    rows = field_ref.shape[0]
    devices = moment_ref.shape[0]

    def moment(place):
        half = place // 8
        value = moment_ref[:, half * LANES : (half + 1) * LANES]
        shift = (LANES - columns * (place % 8)) % LANES
        if shift:
            value = pltpu.roll(value, shift, 1)
        return value.reshape(devices // 8, 8, LANES)

    def total(value):
        value = jnp.sum(value, axis=0)
        width = groups
        while width < 8:
            value = value + pltpu.roll(value, width, 0)
            width *= 2
        return value

    norm = total(moment(0))
    bend = total(moment(1))
    first_step = norm / bend
    change = first_step[None] - moment(12)
    square = moment(4)
    mixed = moment(3)
    norm_next = total(moment(2) - 2.0 * change * mixed + change * change * square)
    drift = total(mixed - change * square)
    curve = total(
        moment(5) - change * moment(6) + change * change * moment(7)
        - first_step[None] * (moment(8) - change * moment(9))
    )
    ratio = norm_next / norm
    bend_next = curve + 2.0 * ratio * drift + ratio * ratio * bend
    second_step = norm_next / bend_next
    on_field = first_step + second_step * (1.0 + ratio)
    on_image = -second_step * first_step
    gradient = on_field * total(moment(10)) + on_image * total(moment(11))
    lane = lax.broadcasted_iota(jnp.int32, (8, LANES), 1)
    row = lax.broadcasted_iota(jnp.int32, (8, LANES), 0)
    counted = jnp.where((lane < columns) & (row < groups), gradient * gradient, 0.0)
    square_total = jnp.sum(jnp.sum(counted, axis=1, keepdims=True), axis=0, keepdims=True)
    scaled = gradient / jnp.sqrt(square_total / (columns * groups) + 1e-06)
    mine = row == place_ref[0]

    def own(value):
        return jnp.sum(jnp.where(mine, value, 0.0), axis=0, keepdims=True)

    step_ref[...] = own(scaled)[:, :columns]
    pair = jnp.concatenate([own(on_field), own(on_image), jnp.zeros((LANES - 2, LANES), jnp.float32)], axis=0)
    flipped = jnp.transpose(pair)[:columns]
    field_rows = jnp.concatenate([jnp.broadcast_to(flipped[:, 0:1], (columns, LANES))] * (rows // columns), axis=0)
    image_rows = jnp.concatenate([jnp.broadcast_to(flipped[:, 1:2], (columns, LANES))] * (rows // columns), axis=0)
    for index in range(field_ref.shape[1] // LANES):
        field_tile = tile(field_ref, index)
        image_tile = tile(lead_ref if index < NB // 2 else image_ref, index)
        twice_tile = tile(twice_ref, index)
        if index < NB // 2:
            twice_tile = twice_tile + tile(far_received_ref, index)
        where = slice(index * LANES, (index + 1) * LANES)
        solution_ref[:, where] = field_rows * field_tile + image_rows * image_tile
        residual_ref[:, where] = field_tile - field_rows * image_tile - image_rows * twice_tile


def shards(right_side, stiffness, contact, pair_local, pair_partner, pair_count, objective_weight):
    components, columns, nodes = right_side.shape
    rows = components * columns
    patches = nodes // PN
    groups = lax.axis_size("col")
    chain_length = lax.axis_size("dom")
    devices = chain_length * groups
    f32 = jnp.float32
    width = NB * PN
    call = functools.partial(
        pl.pallas_call, compiler_params=pltpu.CompilerParams(vmem_limit_bytes=16 * 1024 * 1024)
    )
    shape = jax.ShapeDtypeStruct
    wide = shape((rows, nodes), f32)
    narrow = shape((rows, width), f32)
    scratch = [pltpu.VMEM((patches + NB, rows, LANES), f32)] * 2
    parts = [shape(block.shape, jnp.bfloat16) for block in (stiffness, stiffness, contact, contact)]

    field_hbm = right_side.reshape(rows, nodes)
    halo = shifted(right_side[:, :, :width], "dom", -1).reshape(rows, width)
    chain = jnp.stack([lax.axis_index("dom").astype(jnp.int32), jnp.int32(chain_length)])
    tables = (pair_local, pair_partner, pair_count, chain)
    field, elastic, stiff_high, stiff_low, contact_high, contact_low = call(
        prepare_kernel,
        out_shape=(wide, wide, *parts),
        in_specs=[HBM] * 3,
        out_specs=(VMEM,) * 6,
        scratch_shapes=[
            pltpu.VMEM(stiffness.shape, f32),
            pltpu.VMEM(contact.shape, f32),
            pltpu.SemaphoreType.DMA((3,)),
        ],
        name="prepare",
    )(*(pltpu.with_memory_space_constraint(value, pltpu.HBM) for value in (field_hbm, stiffness, contact)))
    image, spread, even, odd = call(
        couple_kernel,
        out_shape=(wide, narrow, narrow, narrow),
        in_specs=[SMEM] * 4 + [VMEM] * 5,
        out_specs=(VMEM,) * 4,
        scratch_shapes=scratch,
        name="couple",
    )(*tables, field, elastic, halo, contact_high, contact_low)
    even = swapped(even, "dom", False)
    odd = swapped(odd, "dom", True)
    elastic, sums, trial = call(
        functools.partial(lift_kernel, columns=columns),
        out_shape=(
            shape((rows, nodes - width), f32),
            shape((SUMS * columns, LANES), f32),
            shape((columns, LANES), f32),
        ),
        in_specs=[VMEM] * 5,
        out_specs=(VMEM,) * 3,
        name="lift",
    )(field, image, stiff_high, stiff_low, objective_weight)
    twice, lead, moments, far_spread = call(
        functools.partial(second_kernel, columns=columns),
        out_shape=(wide, narrow, shape((devices, 1, MOMENT_LANES), f32), narrow),
        in_specs=[SMEM] * 4 + [VMEM] * 14,
        out_specs=(VMEM,) * 4,
        scratch_shapes=scratch,
        name="second",
    )(
        *tables, field, halo, image, spread, even, odd, stiff_high, stiff_low, contact_high, contact_low,
        objective_weight, sums, trial, elastic,
    )
    gathered = lax.all_to_all(moments, ("dom", "col"), 0, 0, tiled=True).reshape(devices, MOMENT_LANES)
    far_spread = call(relay_kernel, out_shape=narrow, in_specs=[VMEM], out_specs=VMEM, name="relay")(far_spread)
    far_received = shifted(far_spread, "dom", 1)
    place = lax.axis_index("col").astype(jnp.int32).reshape(1)
    solution_field, residual, step = call(
        functools.partial(last_kernel, columns=columns, groups=groups),
        out_shape=(wide, wide, shape((1, columns), f32)),
        in_specs=[SMEM] + [VMEM] * 6,
        out_specs=(VMEM,) * 3,
        name="last",
    )(place, gathered, field, image, lead, twice, far_received)
    return (
        solution_field.reshape(right_side.shape),
        residual.reshape(right_side.shape),
        step.reshape(columns),
    )


def solution(mesh):
    placed = (
        P(None, "col", "dom"),
        P(None, "dom"),
        P(None, "dom"),
        P("dom"),
        P("dom"),
        P("dom"),
        P(None, "dom"),
    )
    return jax.shard_map(
        shards,
        mesh=mesh,
        in_specs=placed,
        out_specs=(P(None, "col", "dom"), P(None, "col", "dom"), P("col")),
        check_vma=False,
    )
```

```python
import functools

import jax
import jax.numpy as jnp
from jax import lax
from jax.experimental import pallas as pl
from jax.experimental.pallas import tpu as pltpu
from jax.sharding import PartitionSpec as P

PN = 64
NB = 8
LANES = 128
MOMENT_LANES = 256
VMEM = pl.BlockSpec(memory_space=pltpu.VMEM)
HBM = pl.BlockSpec(memory_space=pltpu.HBM)
SMEM = pl.BlockSpec(memory_space=pltpu.SMEM)
SUMS = 12
CHUNKS = 4


def shifted(value, axis, by):
    count = lax.axis_size(axis)
    pairs = [(i, i + by) for i in range(count) if 0 <= i + by < count]
    return lax.ppermute(value, axis, pairs)


def swapped(value, axis, odd):
    count = lax.axis_size(axis)
    pairs = []
    for low in range(1 if odd else 0, count, 2):
        high = (low + 1) % count
        pairs += [(low, high), (high, low)]
    return lax.ppermute(value, axis, pairs)


def left_half(shape):
    return lax.broadcasted_iota(jnp.int32, shape, len(shape) - 1) < PN


def split(value):
    high = value.astype(jnp.bfloat16)
    low = (value - high.astype(jnp.float32)).astype(jnp.bfloat16)
    return high, low


def tile(ref, index):
    return ref[:, index * LANES : (index + 1) * LANES]


def put(ref, index, value):
    ref[:, index * LANES : (index + 1) * LANES] = value


def fetch(sources, targets, sems):
    copies = [
        pltpu.make_async_copy(source, target, sems.at[place])
        for place, (source, target) in enumerate(zip(sources, targets))
    ]
    for copy in copies:
        copy.start()
    return copies


def chunked(sources, targets, sems, chunk):
    copies = []
    for start in range(0, targets[0].shape[1], chunk):
        lanes = pl.ds(start, chunk)
        group = []
        for source, target in zip(sources, targets):
            group.append(
                pltpu.make_async_copy(source.at[:, lanes], target.at[:, lanes], sems.at[len(copies) * len(targets) + len(group)])
            )
        copies.append(group)
    return copies


def block_diagonal(high, low):
    mask = left_half((PN, LANES)).astype(jnp.bfloat16)
    other = (1 - left_half((PN, LANES)).astype(jnp.int32)).astype(jnp.bfloat16)
    return (
        jnp.concatenate([high * mask, high * other], axis=0),
        jnp.concatenate([low * mask, low * other], axis=0),
    )


def pair_product(rows, high, low):
    right_high, right_low = block_diagonal(high, low)
    row_high, row_low = split(rows)
    dot = functools.partial(jnp.dot, preferred_element_type=jnp.float32)
    return dot(row_high, right_high) + (dot(row_low, right_high) + dot(row_high, right_low))


def fill_twins(field_tile, twin_ref, patch):
    swapped = pltpu.roll(field_tile, PN, 1)
    left = left_half(field_tile.shape)
    twin_ref[patch] = jnp.where(left, field_tile, swapped)
    twin_ref[patch + 1] = jnp.where(left, swapped, field_tile)


def contacts(twin_ref, high_ref, low_ref, local_ref, partner_ref, count_ref, total_ref):
    rows = twin_ref.shape[1]
    left = left_half((rows, LANES))
    live_count = count_ref[0]
    for step in range(high_ref.shape[1] // LANES):
        slot = 2 * step
        first_a, first_b = local_ref[slot], partner_ref[slot]
        second_a, second_b = local_ref[slot + 1], partner_ref[slot + 1]
        first_live = jnp.where(slot < live_count, 1.0, 0.0)
        second_live = jnp.where(slot + 1 < live_count, 1.0, 0.0)
        first_gap = (twin_ref[first_a] - twin_ref[first_b]) * first_live
        second_gap = (twin_ref[second_a] - twin_ref[second_b]) * second_live
        force = pair_product(
            jnp.where(left, first_gap, second_gap), tile(high_ref, step), tile(low_ref, step)
        )
        first_force = jnp.where(left, force, 0.0)
        second_force = jnp.where(left, 0.0, force)
        total_ref[first_a] = total_ref[first_a] + first_force
        total_ref[first_b] = total_ref[first_b] - first_force
        total_ref[second_a] = total_ref[second_a] + second_force
        total_ref[second_b] = total_ref[second_b] - second_force


def folded(total_ref, patch):
    first, second = total_ref[patch], total_ref[patch + 1]
    first = first + pltpu.roll(first, PN, 1)
    second = second + pltpu.roll(second, PN, 1)
    return jnp.where(left_half(first.shape), first, second)


def clear(total_ref):
    zero = jnp.zeros(total_ref.shape[1:], jnp.float32)
    for patch in range(total_ref.shape[0]):
        total_ref[patch] = zero


def prepare_kernel(
    field_hbm, stiff_hbm, contact_hbm, local_hbm, partner_hbm,
    field_ref, elastic_ref, stiff_high_ref, stiff_low_ref, contact_high_ref, contact_low_ref,
    local_ref, partner_ref,
    stiff_ref, contact_ref, sems, contact_sems, table_sems,
):
    chunk = stiff_ref.shape[1] // CHUNKS
    tiles = chunk // LANES
    copies = chunked((field_hbm, stiff_hbm), (field_ref, stiff_ref), sems, chunk)
    contact_copies = chunked((contact_hbm,), (contact_ref,), contact_sems, chunk)
    for group in copies + contact_copies:
        for copy in group:
            copy.start()
    tables = fetch((local_hbm, partner_hbm), (local_ref, partner_ref), table_sems)
    for place, group in enumerate(copies):
        for copy in group:
            copy.wait()
        for index in range(place * tiles, (place + 1) * tiles):
            high, low = split(tile(stiff_ref, index))
            put(stiff_high_ref, index, high)
            put(stiff_low_ref, index, low)
            put(elastic_ref, index, pair_product(tile(field_ref, index), high, low))
    for place, group in enumerate(contact_copies):
        for copy in group:
            copy.wait()
        for index in range(place * tiles, (place + 1) * tiles):
            high, low = split(tile(contact_ref, index))
            put(contact_high_ref, index, high)
            put(contact_low_ref, index, low)
    for copy in tables:
        copy.wait()


def couple_kernel(
    count_ref, local_vmem, partner_vmem, field_ref, elastic_ref, halo_ref, high_ref, low_ref,
    image_ref, spread_ref, even_ref, odd_ref,
    local_ref, partner_ref, sems, twin_ref, total_ref,
):
    tables = fetch((local_vmem, partner_vmem), (local_ref, partner_ref), sems)
    patches = image_ref.shape[1] // PN
    lead = NB // 2
    clear(total_ref)
    for index in range(patches // 2):
        fill_twins(tile(field_ref, index), twin_ref, 2 * index)
    for index in range(lead):
        fill_twins(tile(halo_ref, index), twin_ref, patches + 2 * index)
    for copy in tables:
        copy.wait()
    contacts(twin_ref, high_ref, low_ref, local_ref, partner_ref, count_ref, total_ref)
    even = lax.axis_index("dom") % 2 == 0
    for index in range(patches // 2):
        value = tile(elastic_ref, index) + folded(total_ref, 2 * index)
        put(image_ref, index, value)
        if index < lead:
            spread = folded(total_ref, patches + 2 * index)
            put(spread_ref, index, spread)
            put(even_ref, index, jnp.where(even, spread, value))
            put(odd_ref, index, jnp.where(even, value, spread))


def by_column(product, columns):
    total = product[:columns]
    for part in range(1, product.shape[0] // columns):
        total = total + product[part * columns : (part + 1) * columns]
    return total


class Sums:
    def __init__(self, columns):
        self.columns = columns
        self.values = {}

    def add(self, place, product):
        product = by_column(product, self.columns)
        self.values[place] = self.values[place] + product if place in self.values else product

    def load(self, ref):
        for place in range(SUMS):
            self.values[place] = ref[place * self.columns : (place + 1) * self.columns]

    def store(self, ref):
        for place in range(SUMS):
            zero = jnp.zeros((self.columns, LANES), jnp.float32)
            ref[place * self.columns : (place + 1) * self.columns] = self.values.get(place, zero)


def weights_of(weight_ref, index, rows):
    parts = weight_ref.shape[0]
    return jnp.concatenate(
        [
            jnp.broadcast_to(weight_ref[part : part + 1, index * LANES : (index + 1) * LANES], (rows // parts, LANES))
            for part in range(parts)
        ],
        axis=0,
    )


def lift_kernel(
    field_ref, image_ref, stiff_high_ref, stiff_low_ref, weight_ref,
    elastic_ref, sums_ref, trial_ref, *, columns,
):
    rows = field_ref.shape[0]
    patches = field_ref.shape[1] // PN
    lead = NB // 2
    sums = Sums(columns)
    for index in range(patches // 2):
        field_tile = tile(field_ref, index)
        weight_tile = weights_of(weight_ref, index, rows)
        sums.add(0, field_tile * field_tile)
        sums.add(10, weight_tile * field_tile)
        if index < lead:
            continue
        image_tile = tile(image_ref, index)
        product = pair_product(image_tile, tile(stiff_high_ref, index), tile(stiff_low_ref, index))
        put(elastic_ref, index - lead, product)
        sums.add(1, field_tile * image_tile)
        sums.add(4, image_tile * image_tile)
        sums.add(11, weight_tile * image_tile)
    across = jnp.sum(sums.values[1], axis=1, keepdims=True)
    square = jnp.sum(sums.values[4], axis=1, keepdims=True)
    some = square > 0.0
    trial = jnp.where(some, across / jnp.where(some, square, 1.0), 0.0)
    trial = jnp.broadcast_to(trial, (columns, LANES))
    trial_ref[...] = trial
    trial_rows = jnp.concatenate([trial] * (rows // columns), axis=0)
    for index in range(lead, patches // 2):
        image_tile = tile(image_ref, index)
        rest = tile(field_ref, index) - trial_rows * image_tile
        sums.add(2, rest * rest)
        sums.add(3, rest * image_tile)
    sums.store(sums_ref)


def second_kernel(
    count_ref, local_vmem, partner_vmem, field_ref, halo_ref, image_ref, spread_ref, even_ref, odd_ref,
    stiff_high_ref, stiff_low_ref, contact_high_ref, contact_low_ref, weight_ref, sums_ref, trial_ref, elastic_ref,
    twice_ref, lead_ref, moment_ref, far_spread_ref,
    local_ref, partner_ref, sems, twin_ref, total_ref, *, columns,
):
    tables = fetch((local_vmem, partner_vmem), (local_ref, partner_ref), sems)
    rows = field_ref.shape[0]
    patches = field_ref.shape[1] // PN
    lead = NB // 2
    place, last = lax.axis_index("dom"), lax.axis_size("dom") - 1
    even = place % 2 == 0
    trial = trial_ref[...]
    trial_rows = jnp.concatenate([trial] * (rows // columns), axis=0)
    sums = Sums(columns)
    sums.load(sums_ref)
    far_tiles = []
    products = []
    clear(total_ref)
    for index in range(lead, patches // 2):
        fill_twins(tile(image_ref, index), twin_ref, 2 * index)
    for index in range(lead):
        first, second = tile(even_ref, index), tile(odd_ref, index)
        received = jnp.where(place > 0, jnp.where(even, second, first), 0.0)
        far_tile = jnp.where(place < last, jnp.where(even, first, second) + tile(spread_ref, index), 0.0)
        far_tiles.append(far_tile)
        fill_twins(far_tile, twin_ref, patches + 2 * index)
        field_tile = tile(field_ref, index)
        image_tile = tile(image_ref, index) + received
        put(lead_ref, index, image_tile)
        fill_twins(image_tile, twin_ref, 2 * index)
        products.append(pair_product(image_tile, tile(stiff_high_ref, index), tile(stiff_low_ref, index)))
        rest = field_tile - trial_rows * image_tile
        sums.add(1, field_tile * image_tile)
        sums.add(2, rest * rest)
        sums.add(3, rest * image_tile)
        sums.add(4, image_tile * image_tile)
        sums.add(11, weights_of(weight_ref, index, rows) * image_tile)
    for copy in tables:
        copy.wait()
    contacts(twin_ref, contact_high_ref, contact_low_ref, local_ref, partner_ref, count_ref, total_ref)
    for index in range(patches // 2):
        image_tile = tile(lead_ref if index < lead else image_ref, index)
        product = products[index] if index < lead else tile(elastic_ref, index - lead)
        twice_tile = product + folded(total_ref, 2 * index)
        put(twice_ref, index, twice_tile)
        rest = tile(field_ref, index) - trial_rows * image_tile
        image_rest = image_tile - trial_rows * twice_tile
        sums.add(5, rest * image_rest)
        sums.add(6, rest * twice_tile + image_tile * image_rest)
        sums.add(7, image_tile * twice_tile)
    for index in range(lead):
        far_spread = folded(total_ref, patches + 2 * index)
        put(far_spread_ref, index, far_spread)
        sums.add(8, (tile(halo_ref, index) - trial_rows * far_tiles[index]) * far_spread)
        sums.add(9, far_tiles[index] * far_spread)
    lane = lax.broadcasted_iota(jnp.int32, (columns, LANES), 1)
    table = jnp.where(lane == SUMS, trial, 0.0)
    for number in range(SUMS):
        table = jnp.where(lane == number, jnp.sum(sums.values[number], axis=1, keepdims=True), table)
    table = jnp.concatenate([table, jnp.zeros((LANES - columns, LANES), jnp.float32)], axis=0)
    flipped = jnp.transpose(table)
    for half in range(2):
        row = pltpu.roll(flipped[half * 8 : half * 8 + 8], 0, 1, stride=columns, stride_axis=0)
        row = jnp.sum(row, axis=0, keepdims=True)
        moment_ref[:, :, half * LANES : (half + 1) * LANES] = jnp.broadcast_to(
            row[None], (moment_ref.shape[0], 1, LANES)
        )


def relay_kernel(value_ref, out_ref):
    out_ref[...] = value_ref[...]


def scale_kernel(moment_ref, scale_ref, step_ref, *, columns, groups):
    devices = moment_ref.shape[0]

    def moment(place):
        half = place // 8
        value = moment_ref[:, half * LANES : (half + 1) * LANES]
        shift = (LANES - columns * (place % 8)) % LANES
        if shift:
            value = pltpu.roll(value, shift, 1)
        return value.reshape(devices // 8, 8, LANES)

    def total(value):
        value = jnp.sum(value, axis=0)
        width = groups
        while width < 8:
            value = value + pltpu.roll(value, width, 0)
            width *= 2
        return value

    norm = total(moment(0))
    bend = total(moment(1))
    first_step = norm / bend
    change = first_step[None] - moment(12)
    square = moment(4)
    mixed = moment(3)
    norm_next = total(moment(2) - 2.0 * change * mixed + change * change * square)
    drift = total(mixed - change * square)
    curve = total(
        moment(5) - change * moment(6) + change * change * moment(7)
        - first_step[None] * (moment(8) - change * moment(9))
    )
    ratio = norm_next / norm
    bend_next = curve + 2.0 * ratio * drift + ratio * ratio * bend
    second_step = norm_next / bend_next
    on_field = first_step + second_step * (1.0 + ratio)
    on_image = -second_step * first_step
    gradient = on_field * total(moment(10)) + on_image * total(moment(11))
    lane = lax.broadcasted_iota(jnp.int32, (8, LANES), 1)
    row = lax.broadcasted_iota(jnp.int32, (8, LANES), 0)
    counted = jnp.where((lane < columns) & (row < groups), gradient * gradient, 0.0)
    square_total = jnp.sum(jnp.sum(counted, axis=1, keepdims=True), axis=0, keepdims=True)
    scaled = gradient / jnp.sqrt(square_total / (columns * groups) + 1e-06)
    mine = row == lax.axis_index("col")

    def own(value):
        return jnp.sum(jnp.where(mine, value, 0.0), axis=0, keepdims=True)

    step_ref[...] = own(scaled)[:, :columns]
    pair = jnp.concatenate([own(on_field), own(on_image), jnp.zeros((LANES - 2, LANES), jnp.float32)], axis=0)
    flipped = jnp.transpose(pair)[:columns]
    scale_ref[:columns] = jnp.broadcast_to(flipped[:, 0:1], (columns, LANES))
    scale_ref[columns:] = jnp.broadcast_to(flipped[:, 1:2], (columns, LANES))


def last_kernel(
    scale_ref, field_ref, image_ref, lead_ref, twice_ref, far_received_ref,
    solution_hbm, residual_hbm, solution_ref, residual_ref, sems,
):
    rows = field_ref.shape[0]
    columns = scale_ref.shape[0] // 2
    field_rows = jnp.concatenate([scale_ref[:columns]] * (rows // columns), axis=0)
    image_rows = jnp.concatenate([scale_ref[columns:]] * (rows // columns), axis=0)
    chunk = field_ref.shape[1] // CHUNKS
    tiles = chunk // LANES
    copies = chunked((solution_ref, residual_ref), (solution_hbm, residual_hbm), sems, chunk)
    for place, group in enumerate(copies):
        for index in range(place * tiles, (place + 1) * tiles):
            field_tile = tile(field_ref, index)
            image_tile = tile(lead_ref if index < NB // 2 else image_ref, index)
            twice_tile = tile(twice_ref, index)
            if index < NB // 2:
                twice_tile = twice_tile + tile(far_received_ref, index)
            put(solution_ref, index, field_rows * field_tile + image_rows * image_tile)
            put(residual_ref, index, field_tile - field_rows * image_tile - image_rows * twice_tile)
        for copy in group:
            copy.start()
    for group in copies:
        for copy in group:
            copy.wait()


def shards(right_side, stiffness, contact, pair_local, pair_partner, pair_count, objective_weight):
    components, columns, nodes = right_side.shape
    rows = components * columns
    patches = nodes // PN
    groups = lax.axis_size("col")
    chain_length = lax.axis_size("dom")
    devices = chain_length * groups
    f32 = jnp.float32
    width = NB * PN
    call = functools.partial(
        pl.pallas_call, compiler_params=pltpu.CompilerParams(vmem_limit_bytes=16 * 1024 * 1024)
    )
    shape = jax.ShapeDtypeStruct
    wide = shape((rows, nodes), f32)
    narrow = shape((rows, width), f32)
    tables = (shape(pair_local.shape, jnp.int32), shape(pair_partner.shape, jnp.int32))
    scratch = [pltpu.SMEM(table.shape, jnp.int32) for table in tables]
    scratch += [pltpu.SemaphoreType.DMA((len(tables),))]
    scratch += [pltpu.VMEM((patches + NB, rows, LANES), f32)] * 2
    parts = [shape(block.shape, jnp.bfloat16) for block in (stiffness, stiffness, contact, contact)]

    field_hbm = right_side.reshape(rows, nodes)
    halo = shifted(right_side[:, :, :width], "dom", -1).reshape(rows, width)
    given = (field_hbm, stiffness, contact, pair_local, pair_partner)
    field, elastic, stiff_high, stiff_low, contact_high, contact_low, *tables = call(
        prepare_kernel,
        out_shape=(wide, wide, *parts, *tables),
        in_specs=[HBM] * 5,
        out_specs=(VMEM,) * 8,
        scratch_shapes=[
            pltpu.VMEM(stiffness.shape, f32),
            pltpu.VMEM(contact.shape, f32),
            pltpu.SemaphoreType.DMA((2 * CHUNKS,)),
            pltpu.SemaphoreType.DMA((CHUNKS,)),
            pltpu.SemaphoreType.DMA((2,)),
        ],
        name="prepare",
    )(*(pltpu.with_memory_space_constraint(value, pltpu.HBM) for value in given))
    image, spread, even, odd = call(
        couple_kernel,
        out_shape=(wide, narrow, narrow, narrow),
        in_specs=[SMEM] + [VMEM] * 7,
        out_specs=(VMEM,) * 4,
        scratch_shapes=scratch,
        name="couple",
    )(pair_count, *tables, field, elastic, halo, contact_high, contact_low)
    even = swapped(even, "dom", False)
    odd = swapped(odd, "dom", True)
    elastic, sums, trial = call(
        functools.partial(lift_kernel, columns=columns),
        out_shape=(
            shape((rows, nodes - width), f32),
            shape((SUMS * columns, LANES), f32),
            shape((columns, LANES), f32),
        ),
        in_specs=[VMEM] * 5,
        out_specs=(VMEM,) * 3,
        name="lift",
    )(field, image, stiff_high, stiff_low, objective_weight)
    twice, lead, moments, far_spread = call(
        functools.partial(second_kernel, columns=columns),
        out_shape=(wide, narrow, shape((devices, 1, MOMENT_LANES), f32), narrow),
        in_specs=[SMEM] + [VMEM] * 16,
        out_specs=(VMEM,) * 4,
        scratch_shapes=scratch,
        name="second",
    )(
        pair_count, *tables, field, halo, image, spread, even, odd, stiff_high, stiff_low, contact_high, contact_low,
        objective_weight, sums, trial, elastic,
    )
    gathered = lax.all_to_all(moments, ("dom", "col"), 0, 0, tiled=True).reshape(devices, MOMENT_LANES)
    far_spread = call(
        relay_kernel,
        out_shape=narrow,
        in_specs=[VMEM],
        out_specs=VMEM,
        cost_estimate=pl.CostEstimate(flops=10**9, bytes_accessed=2 * rows * width * 4, transcendentals=0),
        name="relay",
    )(far_spread)
    far_received = shifted(far_spread, "dom", 1)
    scales, step = call(
        functools.partial(scale_kernel, columns=columns, groups=groups),
        out_shape=(shape((2 * columns, LANES), f32), shape((1, columns), f32)),
        in_specs=[VMEM],
        out_specs=(VMEM,) * 2,
        cost_estimate=pl.CostEstimate(flops=10**9, bytes_accessed=devices * MOMENT_LANES * 4, transcendentals=0),
        name="scale",
    )(gathered)
    solution_field, residual = call(
        last_kernel,
        out_shape=(wide, wide),
        in_specs=[VMEM] * 6,
        out_specs=(HBM,) * 2,
        scratch_shapes=[pltpu.VMEM((rows, nodes), f32)] * 2 + [pltpu.SemaphoreType.DMA((2 * CHUNKS,))],
        name="last",
    )(scales, field, image, lead, twice, far_received)
    return (
        solution_field.reshape(right_side.shape),
        residual.reshape(right_side.shape),
        step.reshape(columns),
    )


def solution(mesh):
    placed = (
        P(None, "col", "dom"),
        P(None, "dom"),
        P(None, "dom"),
        P("dom"),
        P("dom"),
        P("dom"),
        P(None, "dom"),
    )
    return jax.shard_map(
        shards,
        mesh=mesh,
        in_specs=placed,
        out_specs=(P(None, "col", "dom"), P(None, "col", "dom"), P("col")),
        check_vma=False,
    )
```

```python
import functools

import jax
import jax.numpy as jnp
from jax import lax
from jax.experimental import pallas as pl
from jax.experimental.pallas import tpu as pltpu
from jax.sharding import PartitionSpec as P

PN = 64
NB = 8
LANES = 128
MOMENT_LANES = 256
VMEM = pl.BlockSpec(memory_space=pltpu.VMEM)
HBM = pl.BlockSpec(memory_space=pltpu.HBM)
SMEM = pl.BlockSpec(memory_space=pltpu.SMEM)
SUMS = 10
CHUNKS = 4


def shifted(value, axis, by):
    count = lax.axis_size(axis)
    pairs = [(i, i + by) for i in range(count) if 0 <= i + by < count]
    return lax.ppermute(value, axis, pairs)


def swapped(value, odd):
    count, groups = lax.axis_size("dom"), lax.axis_size("col")
    pairs = []
    for place in range(count):
        partner = place + 1 if (place % 2 == 1) == odd else place - 1
        for column in range(groups):
            if 0 <= partner < count:
                pairs.append((place * groups + column, partner * groups + column))
            else:
                beside = column ^ 1 if column ^ 1 < groups else column
                pairs.append((place * groups + column, place * groups + beside))
    return lax.ppermute(value, ("dom", "col"), pairs)


def left_half(shape):
    return lax.broadcasted_iota(jnp.int32, shape, len(shape) - 1) < PN


def split(value):
    high = value.astype(jnp.bfloat16)
    low = (value - high.astype(jnp.float32)).astype(jnp.bfloat16)
    return high, low


def tile(ref, index):
    return ref[:, index * LANES : (index + 1) * LANES]


def put(ref, index, value):
    ref[:, index * LANES : (index + 1) * LANES] = value


def fetch(sources, targets, sems):
    copies = [
        pltpu.make_async_copy(source, target, sems.at[place])
        for place, (source, target) in enumerate(zip(sources, targets))
    ]
    for copy in copies:
        copy.start()
    return copies


def chunked(sources, targets, sems, chunk):
    copies = []
    for start in range(0, targets[0].shape[1], chunk):
        lanes = pl.ds(start, chunk)
        group = []
        for source, target in zip(sources, targets):
            group.append(
                pltpu.make_async_copy(source.at[:, lanes], target.at[:, lanes], sems.at[len(copies) * len(targets) + len(group)])
            )
        copies.append(group)
    return copies


def block_diagonal(high, low):
    mask = left_half((PN, LANES)).astype(jnp.bfloat16)
    other = (1 - left_half((PN, LANES)).astype(jnp.int32)).astype(jnp.bfloat16)
    return (
        jnp.concatenate([high * mask, high * other], axis=0),
        jnp.concatenate([low * mask, low * other], axis=0),
    )


def pair_product(rows, high, low):
    right_high, right_low = block_diagonal(high, low)
    row_high, row_low = split(rows)
    dot = functools.partial(jnp.dot, preferred_element_type=jnp.float32)
    return dot(row_high, right_high) + (dot(row_low, right_high) + dot(row_high, right_low))


def fill_twins(field_tile, twin_ref, patch):
    swapped = pltpu.roll(field_tile, PN, 1)
    left = left_half(field_tile.shape)
    twin_ref[patch] = jnp.where(left, field_tile, swapped)
    twin_ref[patch + 1] = jnp.where(left, swapped, field_tile)


def slot_forces(twin_ref, high_ref, low_ref, local_ref, partner_ref, count_ref, step):
    slot = 2 * step
    live_count = count_ref[0]
    first_live = jnp.where(slot < live_count, 1.0, 0.0)
    second_live = jnp.where(slot + 1 < live_count, 1.0, 0.0)
    first_gap = (twin_ref[local_ref[slot]] - twin_ref[partner_ref[slot]]) * first_live
    second_gap = (twin_ref[local_ref[slot + 1]] - twin_ref[partner_ref[slot + 1]]) * second_live
    gap = jnp.where(left_half(first_gap.shape), first_gap, second_gap)
    return gap, pair_product(gap, tile(high_ref, step), tile(low_ref, step))


def scatter(force, local_ref, partner_ref, total_ref, step):
    slot = 2 * step
    left = left_half(force.shape)
    for number, half in ((slot, jnp.where(left, force, 0.0)), (slot + 1, jnp.where(left, 0.0, force))):
        patch, partner = local_ref[number], partner_ref[number]
        total_ref[patch] = total_ref[patch] + half
        total_ref[partner] = total_ref[partner] - half


def folded(total_ref, patch):
    first, second = total_ref[patch], total_ref[patch + 1]
    first = first + pltpu.roll(first, PN, 1)
    second = second + pltpu.roll(second, PN, 1)
    return jnp.where(left_half(first.shape), first, second)


def clear(total_ref):
    zero = jnp.zeros(total_ref.shape[1:], jnp.float32)
    for patch in range(total_ref.shape[0]):
        total_ref[patch] = zero


def prepare_kernel(
    field_hbm, stiff_hbm, contact_hbm, local_hbm, partner_hbm,
    field_ref, elastic_ref, stiff_high_ref, stiff_low_ref, contact_high_ref, contact_low_ref,
    local_ref, partner_ref,
    stiff_ref, contact_ref, sems, contact_sems, table_sems,
):
    chunk = stiff_ref.shape[1] // CHUNKS
    tiles = chunk // LANES
    copies = chunked((field_hbm, stiff_hbm), (field_ref, stiff_ref), sems, chunk)
    contact_copies = chunked((contact_hbm,), (contact_ref,), contact_sems, chunk)
    for group in copies + contact_copies:
        for copy in group:
            copy.start()
    tables = fetch((local_hbm, partner_hbm), (local_ref, partner_ref), table_sems)
    for place, group in enumerate(copies):
        for copy in group:
            copy.wait()
        for index in range(place * tiles, (place + 1) * tiles):
            high, low = split(tile(stiff_ref, index))
            put(stiff_high_ref, index, high)
            put(stiff_low_ref, index, low)
            put(elastic_ref, index, pair_product(tile(field_ref, index), high, low))
    for place, group in enumerate(contact_copies):
        for copy in group:
            copy.wait()
        for index in range(place * tiles, (place + 1) * tiles):
            high, low = split(tile(contact_ref, index))
            put(contact_high_ref, index, high)
            put(contact_low_ref, index, low)
    for copy in tables:
        copy.wait()


def couple_kernel(
    count_ref, local_vmem, partner_vmem, field_ref, elastic_ref, halo_ref, high_ref, low_ref,
    total_ref, gap_ref, force_ref, own_ref, spread_ref, even_ref, odd_ref,
    local_ref, partner_ref, sems, twin_ref,
):
    tables = fetch((local_vmem, partner_vmem), (local_ref, partner_ref), sems)
    patches = field_ref.shape[1] // PN
    clear(total_ref)
    for index in range(patches // 2):
        fill_twins(tile(field_ref, index), twin_ref, 2 * index)
    for index in range(NB // 2):
        fill_twins(tile(halo_ref, index), twin_ref, patches + 2 * index)
    for copy in tables:
        copy.wait()
    for step in range(high_ref.shape[1] // LANES):
        gap, force = slot_forces(twin_ref, high_ref, low_ref, local_ref, partner_ref, count_ref, step)
        put(gap_ref, step, gap)
        put(force_ref, step, force)
        scatter(force, local_ref, partner_ref, total_ref, step)
    even = lax.axis_index("dom") % 2 == 0
    for index in range(NB // 2):
        value = tile(elastic_ref, index) + folded(total_ref, 2 * index)
        spread = folded(total_ref, patches + 2 * index)
        put(own_ref, index, value)
        put(spread_ref, index, spread)
        put(even_ref, index, jnp.where(even, spread, value))
        put(odd_ref, index, jnp.where(even, value, spread))


def by_column(product, columns):
    total = product[:columns]
    for part in range(1, product.shape[0] // columns):
        total = total + product[part * columns : (part + 1) * columns]
    return total


class Sums:
    def __init__(self, columns):
        self.columns = columns
        self.values = {}

    def add(self, place, product):
        product = by_column(product, self.columns)
        self.values[place] = self.values[place] + product if place in self.values else product

    def load(self, ref):
        for place in range(SUMS):
            self.values[place] = ref[place * self.columns : (place + 1) * self.columns]

    def store(self, ref):
        for place in range(SUMS):
            zero = jnp.zeros((self.columns, LANES), jnp.float32)
            ref[place * self.columns : (place + 1) * self.columns] = self.values.get(place, zero)


def weights_of(weight_ref, index, rows):
    parts = weight_ref.shape[0]
    return jnp.concatenate(
        [
            jnp.broadcast_to(weight_ref[part : part + 1, index * LANES : (index + 1) * LANES], (rows // parts, LANES))
            for part in range(parts)
        ],
        axis=0,
    )


def add_energy(sums, trial_rows, field_part, field_force, image_part, image_force):
    rest = field_part - trial_rows * image_part
    sums.add(5, rest * (field_force - trial_rows * image_force))
    sums.add(6, rest * image_force)
    sums.add(7, image_part * image_force)


def lift_kernel(
    field_ref, total_ref, field_elastic_ref, stiff_high_ref, stiff_low_ref, weight_ref,
    image_ref, elastic_ref, sums_ref, trial_ref, *, columns,
):
    rows = field_ref.shape[0]
    patches = field_ref.shape[1] // PN
    lead = NB // 2
    sums = Sums(columns)
    for index in range(patches // 2):
        field_tile = tile(field_ref, index)
        weight_tile = weights_of(weight_ref, index, rows)
        sums.add(0, field_tile * field_tile)
        sums.add(8, weight_tile * field_tile)
        if index < lead:
            continue
        image_tile = tile(field_elastic_ref, index) + folded(total_ref, 2 * index)
        put(image_ref, index - lead, image_tile)
        product = pair_product(image_tile, tile(stiff_high_ref, index), tile(stiff_low_ref, index))
        put(elastic_ref, index - lead, product)
        sums.add(1, field_tile * image_tile)
        sums.add(4, image_tile * image_tile)
        sums.add(9, weight_tile * image_tile)
    across = jnp.sum(sums.values[1], axis=1, keepdims=True)
    square = jnp.sum(sums.values[4], axis=1, keepdims=True)
    some = square > 0.0
    trial = jnp.where(some, across / jnp.where(some, square, 1.0), 0.0)
    trial = jnp.broadcast_to(trial, (columns, LANES))
    trial_ref[...] = trial
    trial_rows = jnp.concatenate([trial] * (rows // columns), axis=0)
    for index in range(lead, patches // 2):
        field_tile, image_tile = tile(field_ref, index), tile(image_ref, index - lead)
        rest = field_tile - trial_rows * image_tile
        sums.add(2, rest * rest)
        sums.add(3, rest * image_tile)
        add_energy(
            sums, trial_rows, field_tile, tile(field_elastic_ref, index), image_tile, tile(elastic_ref, index - lead)
        )
    sums.store(sums_ref)


def energy_kernel(
    count_ref, local_vmem, partner_vmem, field_ref, field_elastic_ref, gap_ref, force_ref, own_ref, spread_ref,
    even_ref, odd_ref, image_ref, stiff_high_ref, stiff_low_ref, contact_high_ref, contact_low_ref, weight_ref,
    sums_ref, trial_ref,
    lead_ref, lead_elastic_ref, image_force_ref, moment_ref,
    local_ref, partner_ref, sems, twin_ref, *, columns,
):
    tables = fetch((local_vmem, partner_vmem), (local_ref, partner_ref), sems)
    rows = field_ref.shape[0]
    patches = field_ref.shape[1] // PN
    lead = NB // 2
    place, last = lax.axis_index("dom"), lax.axis_size("dom") - 1
    even = place % 2 == 0
    trial = trial_ref[...]
    trial_rows = jnp.concatenate([trial] * (rows // columns), axis=0)
    sums = Sums(columns)
    sums.load(sums_ref)
    for index in range(lead, patches // 2):
        fill_twins(tile(image_ref, index - lead), twin_ref, 2 * index)
    for index in range(lead):
        first, second = tile(even_ref, index), tile(odd_ref, index)
        received = jnp.where(place > 0, jnp.where(even, second, first), 0.0)
        far_tile = jnp.where(place < last, jnp.where(even, first, second) + tile(spread_ref, index), 0.0)
        fill_twins(far_tile, twin_ref, patches + 2 * index)
        field_tile = tile(field_ref, index)
        image_tile = tile(own_ref, index) + received
        put(lead_ref, index, image_tile)
        fill_twins(image_tile, twin_ref, 2 * index)
        product = pair_product(image_tile, tile(stiff_high_ref, index), tile(stiff_low_ref, index))
        put(lead_elastic_ref, index, product)
        rest = field_tile - trial_rows * image_tile
        sums.add(1, field_tile * image_tile)
        sums.add(2, rest * rest)
        sums.add(3, rest * image_tile)
        sums.add(4, image_tile * image_tile)
        sums.add(9, weights_of(weight_ref, index, rows) * image_tile)
        add_energy(sums, trial_rows, field_tile, tile(field_elastic_ref, index), image_tile, product)
    for copy in tables:
        copy.wait()
    for step in range(contact_high_ref.shape[1] // LANES):
        gap, force = slot_forces(
            twin_ref, contact_high_ref, contact_low_ref, local_ref, partner_ref, count_ref, step
        )
        put(image_force_ref, step, force)
        add_energy(sums, trial_rows, tile(gap_ref, step), tile(force_ref, step), gap, force)
    lane = lax.broadcasted_iota(jnp.int32, (columns, LANES), 1)
    table = jnp.where(lane == SUMS, trial, 0.0)
    for number in range(SUMS):
        table = jnp.where(lane == number, jnp.sum(sums.values[number], axis=1, keepdims=True), table)
    table = jnp.concatenate([table, jnp.zeros((LANES - columns, LANES), jnp.float32)], axis=0)
    flipped = jnp.transpose(table)
    for half in range(2):
        row = pltpu.roll(flipped[half * 8 : half * 8 + 8], 0, 1, stride=columns, stride_axis=0)
        row = jnp.sum(row, axis=0, keepdims=True)
        moment_ref[:, :, half * LANES : (half + 1) * LANES] = jnp.broadcast_to(
            row[None], (moment_ref.shape[0], 1, LANES)
        )


def settle_kernel(
    local_vmem, partner_vmem, force_ref,
    total_ref, far_spread_ref,
    local_ref, partner_ref, sems,
):
    tables = fetch((local_vmem, partner_vmem), (local_ref, partner_ref), sems)
    patches = total_ref.shape[0] - NB
    clear(total_ref)
    for copy in tables:
        copy.wait()
    for step in range(force_ref.shape[1] // LANES):
        scatter(tile(force_ref, step), local_ref, partner_ref, total_ref, step)
    for index in range(NB // 2):
        put(far_spread_ref, index, folded(total_ref, patches + 2 * index))


def gather_kernel(total_ref, lead_elastic_ref, elastic_ref, twice_ref):
    lead = NB // 2
    for index in range(twice_ref.shape[1] // LANES):
        product = tile(lead_elastic_ref, index) if index < lead else tile(elastic_ref, index - lead)
        put(twice_ref, index, product + folded(total_ref, 2 * index))


def scale_kernel(moment_ref, scale_ref, step_ref, *, columns, groups):
    devices = moment_ref.shape[0]

    def moment(place):
        half = place // 8
        value = moment_ref[:, half * LANES : (half + 1) * LANES]
        shift = (LANES - columns * (place % 8)) % LANES
        if shift:
            value = pltpu.roll(value, shift, 1)
        return value.reshape(devices // 8, 8, LANES)

    def total(value):
        value = jnp.sum(value, axis=0)
        width = groups
        while width < 8:
            value = value + pltpu.roll(value, width, 0)
            width *= 2
        return value

    norm = total(moment(0))
    bend = total(moment(1))
    first_step = norm / bend
    change = first_step[None] - moment(SUMS)
    square = moment(4)
    mixed = moment(3)
    norm_next = total(moment(2) - 2.0 * change * mixed + change * change * square)
    drift = total(mixed - change * square)
    curve = total(moment(5) - 2.0 * change * moment(6) + change * change * moment(7))
    ratio = norm_next / norm
    bend_next = curve + 2.0 * ratio * drift + ratio * ratio * bend
    second_step = norm_next / bend_next
    on_field = first_step + second_step * (1.0 + ratio)
    on_image = -second_step * first_step
    gradient = on_field * total(moment(8)) + on_image * total(moment(9))
    lane = lax.broadcasted_iota(jnp.int32, (8, LANES), 1)
    row = lax.broadcasted_iota(jnp.int32, (8, LANES), 0)
    counted = jnp.where((lane < columns) & (row < groups), gradient * gradient, 0.0)
    square_total = jnp.sum(jnp.sum(counted, axis=1, keepdims=True), axis=0, keepdims=True)
    scaled = gradient / jnp.sqrt(square_total / (columns * groups) + 1e-06)
    mine = row == lax.axis_index("col")

    def own(value):
        return jnp.sum(jnp.where(mine, value, 0.0), axis=0, keepdims=True)

    step_ref[...] = own(scaled)[:, :columns]
    pair = jnp.concatenate([own(on_field), own(on_image), jnp.zeros((LANES - 2, LANES), jnp.float32)], axis=0)
    flipped = jnp.transpose(pair)[:columns]
    scale_ref[:columns] = jnp.broadcast_to(flipped[:, 0:1], (columns, LANES))
    scale_ref[columns:] = jnp.broadcast_to(flipped[:, 1:2], (columns, LANES))


def last_kernel(
    scale_ref, field_ref, image_ref, lead_ref, twice_ref, far_received_ref,
    solution_hbm, residual_hbm, solution_ref, residual_ref, sems,
):
    rows = field_ref.shape[0]
    columns = scale_ref.shape[0] // 2
    field_rows = jnp.concatenate([scale_ref[:columns]] * (rows // columns), axis=0)
    image_rows = jnp.concatenate([scale_ref[columns:]] * (rows // columns), axis=0)
    chunk = field_ref.shape[1] // CHUNKS
    tiles = chunk // LANES
    copies = chunked((solution_ref, residual_ref), (solution_hbm, residual_hbm), sems, chunk)
    for place, group in enumerate(copies):
        for index in range(place * tiles, (place + 1) * tiles):
            field_tile = tile(field_ref, index)
            image_tile = tile(lead_ref, index) if index < NB // 2 else tile(image_ref, index - NB // 2)
            twice_tile = tile(twice_ref, index)
            if index < NB // 2:
                twice_tile = twice_tile + tile(far_received_ref, index)
            put(solution_ref, index, field_rows * field_tile + image_rows * image_tile)
            put(residual_ref, index, field_tile - field_rows * image_tile - image_rows * twice_tile)
        for copy in group:
            copy.start()
    for group in copies:
        for copy in group:
            copy.wait()


def shards(right_side, stiffness, contact, pair_local, pair_partner, pair_count, objective_weight):
    components, columns, nodes = right_side.shape
    rows = components * columns
    patches = nodes // PN
    groups = lax.axis_size("col")
    chain_length = lax.axis_size("dom")
    devices = chain_length * groups
    f32 = jnp.float32
    width = NB * PN
    call = functools.partial(
        pl.pallas_call, compiler_params=pltpu.CompilerParams(vmem_limit_bytes=8 * 1024 * 1024)
    )
    shape = jax.ShapeDtypeStruct
    wide = shape((rows, nodes), f32)
    narrow = shape((rows, width), f32)
    tables = (shape(pair_local.shape, jnp.int32), shape(pair_partner.shape, jnp.int32))
    scratch = [pltpu.SMEM(table.shape, jnp.int32) for table in tables]
    scratch += [pltpu.SemaphoreType.DMA((len(tables),))]
    twins = pltpu.VMEM((patches + NB, rows, LANES), f32)
    slots = shape((rows, contact.shape[1]), f32)
    parts = [shape(block.shape, jnp.bfloat16) for block in (stiffness, stiffness, contact, contact)]

    field_hbm = right_side.reshape(rows, nodes)
    halo = shifted(right_side[:, :, :width], "dom", -1).reshape(rows, width)
    given = (field_hbm, stiffness, contact, pair_local, pair_partner)
    field, field_elastic, stiff_high, stiff_low, contact_high, contact_low, *tables = call(
        prepare_kernel,
        out_shape=(wide, wide, *parts, *tables),
        in_specs=[HBM] * 5,
        out_specs=(VMEM,) * 8,
        scratch_shapes=[
            pltpu.VMEM(stiffness.shape, f32),
            pltpu.VMEM(contact.shape, f32),
            pltpu.SemaphoreType.DMA((2 * CHUNKS,)),
            pltpu.SemaphoreType.DMA((CHUNKS,)),
            pltpu.SemaphoreType.DMA((2,)),
        ],
        name="prepare",
    )(*(pltpu.with_memory_space_constraint(value, pltpu.HBM) for value in given))
    total, gap, force, own, spread, even, odd = call(
        couple_kernel,
        out_shape=(shape(twins.shape, f32), slots, slots, narrow, narrow, narrow, narrow),
        in_specs=[SMEM] + [VMEM] * 7,
        out_specs=(VMEM,) * 7,
        scratch_shapes=scratch + [twins],
        name="couple",
    )(pair_count, *tables, field, field_elastic, halo, contact_high, contact_low)
    even = swapped(even, False)
    odd = swapped(odd, True)
    tail = shape((rows, nodes - width), f32)
    image, elastic, sums, trial = call(
        functools.partial(lift_kernel, columns=columns),
        out_shape=(tail, tail, shape((SUMS * columns, LANES), f32), shape((columns, LANES), f32)),
        in_specs=[VMEM] * 6,
        out_specs=(VMEM,) * 4,
        name="lift",
    )(field, total, field_elastic, stiff_high, stiff_low, objective_weight)
    lead, lead_elastic, image_force, moments = call(
        functools.partial(energy_kernel, columns=columns),
        out_shape=(narrow, narrow, slots, shape((devices, 1, MOMENT_LANES), f32)),
        in_specs=[SMEM] + [VMEM] * 18,
        out_specs=(VMEM,) * 4,
        scratch_shapes=scratch + [twins],
        name="energy",
    )(
        pair_count, *tables, field, field_elastic, gap, force, own, spread, even, odd, image,
        stiff_high, stiff_low, contact_high, contact_low, objective_weight, sums, trial,
    )
    gathered = lax.all_to_all(moments, ("dom", "col"), 0, 0, tiled=True).reshape(devices, MOMENT_LANES)
    total, far_spread = call(
        settle_kernel,
        out_shape=(shape(twins.shape, f32), narrow),
        in_specs=[VMEM] * 3,
        out_specs=(VMEM,) * 2,
        scratch_shapes=scratch,
        cost_estimate=pl.CostEstimate(flops=10**9, bytes_accessed=4 * rows * nodes * 4, transcendentals=0),
        name="settle",
    )(*tables, image_force)
    far_received = shifted(far_spread, "dom", 1)
    twice = call(
        gather_kernel,
        out_shape=wide,
        in_specs=[VMEM] * 3,
        out_specs=VMEM,
        cost_estimate=pl.CostEstimate(flops=10**9, bytes_accessed=3 * rows * nodes * 4, transcendentals=0),
        name="gather",
    )(total, lead_elastic, elastic)
    scales, step = call(
        functools.partial(scale_kernel, columns=columns, groups=groups),
        out_shape=(shape((2 * columns, LANES), f32), shape((1, columns), f32)),
        in_specs=[VMEM],
        out_specs=(VMEM,) * 2,
        cost_estimate=pl.CostEstimate(flops=10**9, bytes_accessed=devices * MOMENT_LANES * 4, transcendentals=0),
        name="scale",
    )(gathered)
    solution_field, residual = call(
        last_kernel,
        out_shape=(wide, wide),
        in_specs=[VMEM] * 6,
        out_specs=(HBM,) * 2,
        scratch_shapes=[pltpu.VMEM((rows, nodes), f32)] * 2 + [pltpu.SemaphoreType.DMA((2 * CHUNKS,))],
        name="last",
    )(scales, field, image, lead, twice, far_received)
    return (
        solution_field.reshape(right_side.shape),
        residual.reshape(right_side.shape),
        step.reshape(columns),
    )


def solution(mesh):
    placed = (
        P(None, "col", "dom"),
        P(None, "dom"),
        P(None, "dom"),
        P("dom"),
        P("dom"),
        P("dom"),
        P(None, "dom"),
    )
    return jax.shard_map(
        shards,
        mesh=mesh,
        in_specs=placed,
        out_specs=(P(None, "col", "dom"), P(None, "col", "dom"), P("col")),
        check_vma=False,
    )
```

```python
import functools

import jax
import jax.numpy as jnp
from jax import lax
from jax.experimental import pallas as pl
from jax.experimental.pallas import tpu as pltpu
from jax.sharding import PartitionSpec as P

PN = 64
NB = 8
LANES = 128
SMEM = pl.BlockSpec(memory_space=pltpu.SMEM)
MOMENT_LANES = 256
VMEM = pl.BlockSpec(memory_space=pltpu.VMEM)
HBM = pl.BlockSpec(memory_space=pltpu.HBM)
SUMS = 10
CHUNKS = 4
LAST_CHUNKS = 4


def shifted(value, axis, by):
    count = lax.axis_size(axis)
    pairs = [(i, i + by) for i in range(count) if 0 <= i + by < count]
    return lax.ppermute(value, axis, pairs)


def swapped(value, odd):
    count, groups = lax.axis_size("dom"), lax.axis_size("col")
    pairs = []
    for place in range(count):
        partner = place + 1 if (place % 2 == 1) == odd else place - 1
        for column in range(groups):
            if 0 <= partner < count:
                pairs.append((place * groups + column, partner * groups + column))
            else:
                beside = column ^ 1 if column ^ 1 < groups else column
                pairs.append((place * groups + column, place * groups + beside))
    return lax.ppermute(value, ("dom", "col"), pairs)


def left_half(shape):
    return lax.broadcasted_iota(jnp.int32, shape, len(shape) - 1) < PN


def split(value):
    high = value.astype(jnp.bfloat16)
    low = (value - high.astype(jnp.float32)).astype(jnp.bfloat16)
    return high, low


def tile(ref, index):
    return ref[:, index * LANES : (index + 1) * LANES]


def put(ref, index, value):
    ref[:, index * LANES : (index + 1) * LANES] = value


class Slots:
    def __init__(self, sources, targets, sems):
        self.local, self.partner = targets
        self.copies = [
            pltpu.make_async_copy(source, target, sems.at[place])
            for place, (source, target) in enumerate(zip(sources, targets))
        ]
        for copy in self.copies:
            copy.start()

    def wait(self):
        for copy in self.copies:
            copy.wait()


def live(count_ref, slot):
    return jnp.where(slot < count_ref[0], 1.0, 0.0)


def chunked(sources, targets, sems, chunk):
    copies = []
    for start in range(0, targets[0].shape[1], chunk):
        lanes = pl.ds(start, chunk)
        group = []
        for source, target in zip(sources, targets):
            group.append(
                pltpu.make_async_copy(source.at[:, lanes], target.at[:, lanes], sems.at[len(copies) * len(targets) + len(group)])
            )
        copies.append(group)
    return copies


def block_diagonal(high, low):
    mask = left_half((PN, LANES)).astype(jnp.bfloat16)
    other = (1 - left_half((PN, LANES)).astype(jnp.int32)).astype(jnp.bfloat16)
    return (
        jnp.concatenate([high * mask, high * other], axis=0),
        jnp.concatenate([low * mask, low * other], axis=0),
    )


def pair_product(rows, high, low):
    right_high, right_low = block_diagonal(high, low)
    row_high, row_low = split(rows)
    dot = functools.partial(jnp.dot, preferred_element_type=jnp.float32)
    return dot(row_high, right_high) + (dot(row_low, right_high) + dot(row_high, right_low))


def fill_twins(field_tile, twin_ref, patch):
    swapped = pltpu.roll(field_tile, PN, 1)
    left = left_half(field_tile.shape)
    twin_ref[patch] = jnp.where(left, field_tile, swapped)
    twin_ref[patch + 1] = jnp.where(left, swapped, field_tile)


def side_by_side(first, second):
    return jnp.where(left_half(first.shape), first, second)


def scatter(force, step, targets):
    left = left_half(force.shape)
    for slot, half in ((2 * step, jnp.where(left, force, 0.0)), (2 * step + 1, jnp.where(left, 0.0, force))):
        for ref, patch, sign in targets(slot):
            ref[patch] = ref[patch] + half if sign > 0 else ref[patch] - half


def folded(total_ref, patch):
    first, second = total_ref[patch], total_ref[patch + 1]
    first = first + pltpu.roll(first, PN, 1)
    second = second + pltpu.roll(second, PN, 1)
    return jnp.where(left_half(first.shape), first, second)


def clear(total_ref):
    zero = jnp.zeros(total_ref.shape[1:], jnp.float32)
    for patch in range(total_ref.shape[0]):
        total_ref[patch] = zero


def prepare_kernel(
    field_hbm, stiff_hbm, contact_hbm, local_hbm, partner_hbm,
    field_ref, elastic_ref, stiff_high_ref, stiff_low_ref, contact_high_ref, contact_low_ref, local_ref, partner_ref,
    stiff_ref, contact_ref, sems, contact_sems, table_sems,
):
    chunk = stiff_ref.shape[1] // CHUNKS
    tiles = chunk // LANES
    copies = chunked((field_hbm, stiff_hbm), (field_ref, stiff_ref), sems, chunk)
    contact_copies = chunked((contact_hbm,), (contact_ref,), contact_sems, chunk)
    for group in copies + contact_copies:
        for copy in group:
            copy.start()
    slots = Slots((local_hbm, partner_hbm), (local_ref, partner_ref), table_sems)
    for place, group in enumerate(copies):
        for copy in group:
            copy.wait()
        for index in range(place * tiles, (place + 1) * tiles):
            high, low = split(tile(stiff_ref, index))
            put(stiff_high_ref, index, high)
            put(stiff_low_ref, index, low)
            put(elastic_ref, index, pair_product(tile(field_ref, index), high, low))
    for place, group in enumerate(contact_copies):
        for copy in group:
            copy.wait()
        for index in range(place * tiles, (place + 1) * tiles):
            high, low = split(tile(contact_ref, index))
            put(contact_high_ref, index, high)
            put(contact_low_ref, index, low)
    slots.wait()


def couple_kernel(
    count_ref, local_vmem, partner_vmem, field_ref, elastic_ref, halo_ref, high_ref, low_ref,
    total_ref, gap_ref, force_ref, own_ref, spread_ref, even_ref, odd_ref,
    local_ref, partner_ref, table_sems, twin_ref,
):
    slots = Slots((local_vmem, partner_vmem), (local_ref, partner_ref), table_sems)
    patches = field_ref.shape[1] // PN
    clear(total_ref)
    for index in range(patches // 2):
        fill_twins(tile(field_ref, index), twin_ref, 2 * index)
    for index in range(NB // 2):
        fill_twins(tile(halo_ref, index), twin_ref, patches + 2 * index)
    slots.wait()

    def slot_gap(slot):
        return (twin_ref[slots.local[slot]] - twin_ref[slots.partner[slot]]) * live(count_ref, slot)

    def targets(slot):
        return (total_ref, slots.local[slot], 1), (total_ref, slots.partner[slot], -1)

    for step in range(high_ref.shape[1] // LANES):
        gap = side_by_side(slot_gap(2 * step), slot_gap(2 * step + 1))
        force = pair_product(gap, tile(high_ref, step), tile(low_ref, step))
        put(gap_ref, step, gap)
        put(force_ref, step, force)
        scatter(force, step, targets)
    even = lax.axis_index("dom") % 2 == 0
    for index in range(NB // 2):
        value = tile(elastic_ref, index) + folded(total_ref, 2 * index)
        spread = folded(total_ref, patches + 2 * index)
        put(own_ref, index, value)
        put(spread_ref, index, spread)
        put(even_ref, index, jnp.where(even, spread, value))
        put(odd_ref, index, jnp.where(even, value, spread))


def by_column(product, columns):
    total = product[:columns]
    for part in range(1, product.shape[0] // columns):
        total = total + product[part * columns : (part + 1) * columns]
    return total


class Sums:
    def __init__(self, columns):
        self.columns = columns
        self.values = {}

    def add(self, place, product):
        product = by_column(product, self.columns)
        self.values[place] = self.values[place] + product if place in self.values else product

    def load(self, ref):
        for place in range(SUMS):
            self.values[place] = ref[place * self.columns : (place + 1) * self.columns]

    def store(self, ref):
        for place in range(SUMS):
            zero = jnp.zeros((self.columns, LANES), jnp.float32)
            ref[place * self.columns : (place + 1) * self.columns] = self.values.get(place, zero)


def weights_of(weight_ref, index, rows):
    parts = weight_ref.shape[0]
    return jnp.concatenate(
        [
            jnp.broadcast_to(weight_ref[part : part + 1, index * LANES : (index + 1) * LANES], (rows // parts, LANES))
            for part in range(parts)
        ],
        axis=0,
    )


def add_energy(sums, trial_rows, field_part, field_force, image_part, image_force):
    rest = field_part - trial_rows * image_part
    sums.add(5, rest * (field_force - trial_rows * image_force))
    sums.add(6, rest * image_force)
    sums.add(7, image_part * image_force)


def lift_kernel(
    local_vmem, partner_vmem, field_ref, total_ref, field_elastic_ref, stiff_high_ref, stiff_low_ref, weight_ref,
    image_ref, elastic_ref, near_ref, sums_ref, trial_ref,
    local_ref, partner_ref, table_sems, twin_ref, *, columns,
):
    slots = Slots((local_vmem, partner_vmem), (local_ref, partner_ref), table_sems)
    rows = field_ref.shape[0]
    patches = field_ref.shape[1] // PN
    lead = NB // 2
    sums = Sums(columns)
    for index in range(patches // 2):
        field_tile = tile(field_ref, index)
        weight_tile = weights_of(weight_ref, index, rows)
        sums.add(0, field_tile * field_tile)
        sums.add(8, weight_tile * field_tile)
        if index < lead:
            continue
        image_tile = tile(field_elastic_ref, index) + folded(total_ref, 2 * index)
        put(image_ref, index - lead, image_tile)
        fill_twins(image_tile, twin_ref, 2 * index)
        product = pair_product(image_tile, tile(stiff_high_ref, index), tile(stiff_low_ref, index))
        put(elastic_ref, index - lead, product)
        sums.add(1, field_tile * image_tile)
        sums.add(4, image_tile * image_tile)
        sums.add(9, weight_tile * image_tile)
    across = jnp.sum(sums.values[1], axis=1, keepdims=True)
    square = jnp.sum(sums.values[4], axis=1, keepdims=True)
    some = square > 0.0
    trial = jnp.where(some, across / jnp.where(some, square, 1.0), 0.0)
    trial = jnp.broadcast_to(trial, (columns, LANES))
    trial_ref[...] = trial
    trial_rows = jnp.concatenate([trial] * (rows // columns), axis=0)
    for index in range(lead, patches // 2):
        field_tile, image_tile = tile(field_ref, index), tile(image_ref, index - lead)
        rest = field_tile - trial_rows * image_tile
        sums.add(2, rest * rest)
        sums.add(3, rest * image_tile)
        add_energy(
            sums, trial_rows, field_tile, tile(field_elastic_ref, index), image_tile, tile(elastic_ref, index - lead)
        )
    sums.store(sums_ref)
    twin_ref[patches] = jnp.zeros(twin_ref.shape[1:], jnp.float32)
    slots.wait()

    def inner(patch):
        return twin_ref[jnp.where((patch >= NB) & (patch < patches), patch, patches)]

    def inner_gap(slot):
        return inner(slots.local[slot]) - inner(slots.partner[slot])

    for step in range(near_ref.shape[1] // LANES):
        put(near_ref, step, side_by_side(inner_gap(2 * step), inner_gap(2 * step + 1)))


def energy_kernel(
    count_ref, local_vmem, partner_vmem, field_ref, field_elastic_ref, gap_ref, force_ref, own_ref, spread_ref,
    even_ref, odd_ref, near_ref, stiff_high_ref, stiff_low_ref, contact_high_ref, contact_low_ref, weight_ref,
    sums_ref, trial_ref,
    lead_ref, lead_elastic_ref, image_force_ref, moment_ref,
    local_ref, partner_ref, table_sems, twin_ref, *, columns,
):
    slots = Slots((local_vmem, partner_vmem), (local_ref, partner_ref), table_sems)
    rows = field_ref.shape[0]
    patches = field_ref.shape[1] // PN
    lead = NB // 2
    place, last = lax.axis_index("dom"), lax.axis_size("dom") - 1
    even = place % 2 == 0
    trial = trial_ref[...]
    trial_rows = jnp.concatenate([trial] * (rows // columns), axis=0)
    sums = Sums(columns)
    sums.load(sums_ref)
    for index in range(lead):
        first, second = tile(even_ref, index), tile(odd_ref, index)
        received = jnp.where(place > 0, jnp.where(even, second, first), 0.0)
        far_tile = jnp.where(place < last, jnp.where(even, first, second) + tile(spread_ref, index), 0.0)
        fill_twins(far_tile, twin_ref, NB + 2 * index)
        field_tile = tile(field_ref, index)
        image_tile = tile(own_ref, index) + received
        put(lead_ref, index, image_tile)
        fill_twins(image_tile, twin_ref, 2 * index)
        product = pair_product(image_tile, tile(stiff_high_ref, index), tile(stiff_low_ref, index))
        put(lead_elastic_ref, index, product)
        rest = field_tile - trial_rows * image_tile
        sums.add(1, field_tile * image_tile)
        sums.add(2, rest * rest)
        sums.add(3, rest * image_tile)
        sums.add(4, image_tile * image_tile)
        sums.add(9, weights_of(weight_ref, index, rows) * image_tile)
        add_energy(sums, trial_rows, field_tile, tile(field_elastic_ref, index), image_tile, product)
    twin_ref[2 * NB] = jnp.zeros(twin_ref.shape[1:], jnp.float32)
    slots.wait()

    def outer(patch):
        far = patch >= patches
        return twin_ref[jnp.where(far, patch - patches + NB, jnp.where(patch < NB, patch, 2 * NB))]

    def outer_gap(slot):
        return outer(slots.local[slot]) - outer(slots.partner[slot])

    for step in range(contact_high_ref.shape[1] // LANES):
        gap = tile(near_ref, step) + side_by_side(outer_gap(2 * step), outer_gap(2 * step + 1))
        lives = [jnp.full(gap.shape, live(count_ref, 2 * step + side), jnp.float32) for side in range(2)]
        gap = gap * side_by_side(*lives)
        force = pair_product(gap, tile(contact_high_ref, step), tile(contact_low_ref, step))
        put(image_force_ref, step, force)
        add_energy(sums, trial_rows, tile(gap_ref, step), tile(force_ref, step), gap, force)
    lane = lax.broadcasted_iota(jnp.int32, (columns, LANES), 1)
    column = lax.broadcasted_iota(jnp.int32, (columns, LANES), 0)
    for half in range(2):
        spread_out = jnp.zeros((columns, LANES), jnp.float32)
        for number in range(half * 8, min(half * 8 + 8, SUMS + 1)):
            value = trial if number == SUMS else jnp.sum(sums.values[number], axis=1, keepdims=True)
            spread_out = jnp.where(lane == column + columns * (number % 8), value, spread_out)
        row = jnp.sum(spread_out, axis=0, keepdims=True)
        moment_ref[:, :, half * LANES : (half + 1) * LANES] = jnp.broadcast_to(
            row[None], (moment_ref.shape[0], 1, LANES)
        )


def settle_kernel(
    local_vmem, partner_vmem, force_ref, far_spread_ref, local_ref, partner_ref, table_sems, total_ref, *, patches
):
    slots = Slots((local_vmem, partner_vmem), (local_ref, partner_ref), table_sems)
    clear(total_ref)
    slots.wait()

    def targets(slot):
        partner = slots.partner[slot]
        return ((total_ref, jnp.where(partner < patches, NB, partner - patches), -1),)

    for step in range(force_ref.shape[1] // LANES):
        scatter(tile(force_ref, step), step, targets)
    for index in range(NB // 2):
        put(far_spread_ref, index, folded(total_ref, 2 * index))


def gather_kernel(
    local_vmem, partner_vmem, force_ref, lead_elastic_ref, elastic_ref, twice_ref,
    local_ref, partner_ref, table_sems, total_ref,
):
    slots = Slots((local_vmem, partner_vmem), (local_ref, partner_ref), table_sems)
    patches = twice_ref.shape[1] // PN
    lead = NB // 2
    clear(total_ref)
    slots.wait()

    def targets(slot):
        partner = slots.partner[slot]
        return (total_ref, slots.local[slot], 1), (total_ref, jnp.where(partner < patches, partner, patches), -1)

    for step in range(force_ref.shape[1] // LANES):
        scatter(tile(force_ref, step), step, targets)
    for index in range(patches // 2):
        product = tile(lead_elastic_ref, index) if index < lead else tile(elastic_ref, index - lead)
        put(twice_ref, index, product + folded(total_ref, 2 * index))


def scale_kernel(moment_ref, scale_ref, gradient_ref, *, columns, groups):
    devices = moment_ref.shape[0]

    def moment(place):
        half = place // 8
        value = moment_ref[:, half * LANES : (half + 1) * LANES]
        shift = (LANES - columns * (place % 8)) % LANES
        if shift:
            value = pltpu.roll(value, shift, 1)
        return value.reshape(devices // 8, 8, LANES)

    def total(value):
        value = jnp.sum(value, axis=0)
        width = groups
        while width < 8:
            value = value + pltpu.roll(value, width, 0)
            width *= 2
        return value

    norm = total(moment(0))
    bend = total(moment(1))
    first_step = norm / bend
    change = first_step[None] - moment(SUMS)
    square = moment(4)
    mixed = moment(3)
    norm_next = total(moment(2) - 2.0 * change * mixed + change * change * square)
    drift = total(mixed - change * square)
    curve = total(moment(5) - 2.0 * change * moment(6) + change * change * moment(7))
    ratio = norm_next / norm
    bend_next = curve + 2.0 * ratio * drift + ratio * ratio * bend
    second_step = norm_next / bend_next
    on_field = first_step + second_step * (1.0 + ratio)
    on_image = -second_step * first_step
    gradient = on_field * total(moment(8)) + on_image * total(moment(9))
    gradient_ref[...] = gradient
    mine = lax.broadcasted_iota(jnp.int32, (8, LANES), 0) == lax.axis_index("col")
    diagonal = lax.broadcasted_iota(jnp.int32, (columns, LANES), 0) == lax.broadcasted_iota(
        jnp.int32, (columns, LANES), 1
    )
    for place, value in enumerate((on_field, on_image)):
        own = jnp.sum(jnp.where(mine, value, 0.0), axis=0, keepdims=True)
        own = jnp.sum(jnp.where(diagonal, own, 0.0), axis=1, keepdims=True)
        scale_ref[place * columns : (place + 1) * columns] = jnp.broadcast_to(own, (columns, LANES))


def own_step(gradient, columns, groups):
    lane = lax.broadcasted_iota(jnp.int32, (8, LANES), 1)
    row = lax.broadcasted_iota(jnp.int32, (8, LANES), 0)
    counted = jnp.where((lane < columns) & (row < groups), gradient * gradient, 0.0)
    square_total = jnp.sum(jnp.sum(counted, axis=1, keepdims=True), axis=0, keepdims=True)
    scaled = gradient / jnp.sqrt(square_total / (columns * groups) + 1e-06)
    return jnp.sum(jnp.where(row == lax.axis_index("col"), scaled, 0.0), axis=0, keepdims=True)[:, :columns]


def scale_rows(scale_ref, rows):
    columns = scale_ref.shape[0] // 2
    return (
        jnp.concatenate([scale_ref[:columns]] * (rows // columns), axis=0),
        jnp.concatenate([scale_ref[columns:]] * (rows // columns), axis=0),
    )


def last_kernel(
    scale_ref, gradient_ref, field_ref, image_ref, lead_ref, twice_ref, far_received_ref,
    solution_hbm, residual_hbm, step_hbm, solution_ref, residual_ref, step_ref, sems, step_sem, *, groups,
):
    field_rows, image_rows = scale_rows(scale_ref, field_ref.shape[0])
    chunk = field_ref.shape[1] // LAST_CHUNKS
    tiles = chunk // LANES
    copies = chunked((solution_ref, residual_ref), (solution_hbm, residual_hbm), sems, chunk)
    step_copy = pltpu.make_async_copy(step_ref, step_hbm, step_sem.at[0])
    for place, group in enumerate(copies):
        for index in range(place * tiles, (place + 1) * tiles):
            field_tile = tile(field_ref, index)
            image_tile = tile(lead_ref, index) if index < NB // 2 else tile(image_ref, index - NB // 2)
            twice_tile = tile(twice_ref, index)
            if index < NB // 2:
                twice_tile = twice_tile + tile(far_received_ref, index)
            put(solution_ref, index, field_rows * field_tile + image_rows * image_tile)
            put(residual_ref, index, field_tile - field_rows * image_tile - image_rows * twice_tile)
        for copy in group:
            copy.start()
        if place == 0:
            step_ref[...] = own_step(gradient_ref[...], scale_ref.shape[0] // 2, groups)
            step_copy.start()
    step_copy.wait()
    for group in copies:
        for copy in group:
            copy.wait()


def shards(right_side, stiffness, contact, pair_local, pair_partner, pair_count, objective_weight):
    components, columns, nodes = right_side.shape
    rows = components * columns
    patches = nodes // PN
    groups = lax.axis_size("col")
    chain_length = lax.axis_size("dom")
    devices = chain_length * groups
    f32 = jnp.float32
    width = NB * PN
    call = functools.partial(
        pl.pallas_call, compiler_params=pltpu.CompilerParams(vmem_limit_bytes=8 * 1024 * 1024)
    )
    shape = jax.ShapeDtypeStruct
    wide = shape((rows, nodes), f32)
    narrow = shape((rows, width), f32)
    parts = [shape(block.shape, jnp.bfloat16) for block in (stiffness, stiffness, contact, contact)]

    def in_hbm(value):
        return pltpu.with_memory_space_constraint(value, pltpu.HBM)

    field_hbm = in_hbm(right_side.reshape(rows, nodes))
    pairs = (in_hbm(pair_local), in_hbm(pair_partner))
    slots = shape((rows, contact.shape[1]), f32)

    def scratch(count):
        return [
            pltpu.SMEM(pair_local.shape, jnp.int32),
            pltpu.SMEM(pair_partner.shape, jnp.int32),
            pltpu.SemaphoreType.DMA((2,)),
            pltpu.VMEM((count, rows, LANES), f32),
        ]

    halo = shifted(right_side[:, :, :width], "dom", -1).reshape(rows, width)
    field, field_elastic, stiff_high, stiff_low, contact_high, contact_low, *tables = call(
        prepare_kernel,
        out_shape=(wide, wide, *parts, *(shape(pair.shape, jnp.int32) for pair in pairs)),
        in_specs=[HBM] * 5,
        out_specs=(VMEM,) * 8,
        scratch_shapes=[
            pltpu.VMEM(stiffness.shape, f32),
            pltpu.VMEM(contact.shape, f32),
            pltpu.SemaphoreType.DMA((2 * CHUNKS,)),
            pltpu.SemaphoreType.DMA((CHUNKS,)),
            pltpu.SemaphoreType.DMA((2,)),
        ],
        name="prepare",
    )(field_hbm, in_hbm(stiffness), in_hbm(contact), *pairs)
    total, gap, force, own, spread, even, odd = call(
        couple_kernel,
        out_shape=(shape((patches + NB, rows, LANES), f32), slots, slots, narrow, narrow, narrow, narrow),
        in_specs=[SMEM] + [VMEM] * 7,
        out_specs=(VMEM,) * 7,
        scratch_shapes=scratch(patches + NB),
        name="couple",
    )(pair_count, *tables, field, field_elastic, halo, contact_high, contact_low)
    even = swapped(even, False)
    odd = swapped(odd, True)
    tail = shape((rows, nodes - width), f32)
    image, elastic, near, sums, trial = call(
        functools.partial(lift_kernel, columns=columns),
        out_shape=(tail, tail, slots, shape((SUMS * columns, LANES), f32), shape((columns, LANES), f32)),
        in_specs=[VMEM] * 8,
        out_specs=(VMEM,) * 5,
        scratch_shapes=scratch(patches + 1),
        name="lift",
    )(*tables, field, total, field_elastic, stiff_high, stiff_low, objective_weight)
    lead, lead_elastic, image_force, moments = call(
        functools.partial(energy_kernel, columns=columns),
        out_shape=(narrow, narrow, slots, shape((devices, 1, MOMENT_LANES), f32)),
        in_specs=[SMEM] + [VMEM] * 18,
        out_specs=(VMEM,) * 4,
        scratch_shapes=scratch(2 * NB + 1),
        name="energy",
    )(
        pair_count, *tables, field, field_elastic, gap, force, own, spread, even, odd, near,
        stiff_high, stiff_low, contact_high, contact_low, objective_weight, sums, trial,
    )
    gathered = lax.all_to_all(moments, ("dom", "col"), 0, 0, tiled=True).reshape(devices, MOMENT_LANES)
    far_spread = call(
        functools.partial(settle_kernel, patches=patches),
        out_shape=narrow,
        in_specs=[VMEM] * 3,
        out_specs=VMEM,
        scratch_shapes=scratch(NB + 1),
        cost_estimate=pl.CostEstimate(flops=10**9, bytes_accessed=rows * nodes * 4, transcendentals=0),
        name="settle",
    )(*tables, image_force)
    far_received = shifted(far_spread, "dom", 1)
    twice = call(
        gather_kernel,
        out_shape=wide,
        in_specs=[VMEM] * 5,
        out_specs=VMEM,
        scratch_shapes=scratch(patches + 1),
        cost_estimate=pl.CostEstimate(flops=10**9, bytes_accessed=3 * rows * nodes * 4, transcendentals=0),
        name="gather",
    )(*tables, image_force, lead_elastic, elastic)
    scales, gradient = call(
        functools.partial(scale_kernel, columns=columns, groups=groups),
        out_shape=(shape((2 * columns, LANES), f32), shape((8, LANES), f32)),
        in_specs=[VMEM],
        out_specs=(VMEM,) * 2,
        cost_estimate=pl.CostEstimate(flops=10**9, bytes_accessed=devices * MOMENT_LANES * 4, transcendentals=0),
        name="scale",
    )(gathered)
    solution_field, residual, step = call(
        functools.partial(last_kernel, groups=groups),
        out_shape=(wide, wide, shape((1, columns), f32)),
        in_specs=[VMEM] * 7,
        out_specs=(HBM,) * 3,
        scratch_shapes=[pltpu.VMEM((rows, nodes), f32)] * 2
        + [
            pltpu.VMEM((1, columns), f32),
            pltpu.SemaphoreType.DMA((2 * LAST_CHUNKS,)),
            pltpu.SemaphoreType.DMA((1,)),
        ],
        name="last",
    )(scales, gradient, field, image, lead, twice, far_received)
    return (
        solution_field.reshape(right_side.shape),
        residual.reshape(right_side.shape),
        step.reshape(columns),
    )


def solution(mesh):
    placed = (
        P(None, "col", "dom"),
        P(None, "dom"),
        P(None, "dom"),
        P("dom"),
        P("dom"),
        P("dom"),
        P(None, "dom"),
    )
    return jax.shard_map(
        shards,
        mesh=mesh,
        in_specs=placed,
        out_specs=(P(None, "col", "dom"), P(None, "col", "dom"), P("col")),
        check_vma=False,
    )
```

```python
import functools

import jax
import jax.numpy as jnp
from jax import lax
from jax.experimental import pallas as pl
from jax.experimental.pallas import tpu as pltpu
from jax.sharding import PartitionSpec as P

PN = 64
NB = 8
LANES = 128
SMEM = pl.BlockSpec(memory_space=pltpu.SMEM)
MOMENT_LANES = 256
VMEM = pl.BlockSpec(memory_space=pltpu.VMEM)
HBM = pl.BlockSpec(memory_space=pltpu.HBM)
SUMS = 10
CHUNKS = 4
LAST_CHUNKS = 4


def shifted(value, axis, by):
    count = lax.axis_size(axis)
    pairs = [(i, i + by) for i in range(count) if 0 <= i + by < count]
    return lax.ppermute(value, axis, pairs)


def swapped(value, odd):
    count, groups = lax.axis_size("dom"), lax.axis_size("col")
    pairs = []
    for place in range(count):
        partner = place + 1 if (place % 2 == 1) == odd else place - 1
        for column in range(groups):
            if 0 <= partner < count:
                pairs.append((place * groups + column, partner * groups + column))
            else:
                beside = column ^ 1 if column ^ 1 < groups else column
                pairs.append((place * groups + column, place * groups + beside))
    return lax.ppermute(value, ("dom", "col"), pairs)


def left_half(shape):
    return lax.broadcasted_iota(jnp.int32, shape, len(shape) - 1) < PN


def split(value):
    high = value.astype(jnp.bfloat16)
    low = (value - high.astype(jnp.float32)).astype(jnp.bfloat16)
    return high, low


def tile(ref, index):
    return ref[:, index * LANES : (index + 1) * LANES]


def put(ref, index, value):
    ref[:, index * LANES : (index + 1) * LANES] = value


class Slots:
    def __init__(self, sources, targets, sems):
        self.local, self.partner = targets
        self.copies = [
            pltpu.make_async_copy(source, target, sems.at[place])
            for place, (source, target) in enumerate(zip(sources, targets))
        ]
        for copy in self.copies:
            copy.start()

    def wait(self):
        for copy in self.copies:
            copy.wait()


def live(count_ref, slot):
    return jnp.where(slot < count_ref[0], 1.0, 0.0)


def chunked(sources, targets, sems, chunk):
    copies = []
    for start in range(0, targets[0].shape[1], chunk):
        lanes = pl.ds(start, chunk)
        group = []
        for source, target in zip(sources, targets):
            group.append(
                pltpu.make_async_copy(source.at[:, lanes], target.at[:, lanes], sems.at[len(copies) * len(targets) + len(group)])
            )
        copies.append(group)
    return copies


def block_diagonal(high, low):
    mask = left_half((PN, LANES)).astype(jnp.bfloat16)
    other = (1 - left_half((PN, LANES)).astype(jnp.int32)).astype(jnp.bfloat16)
    return (
        jnp.concatenate([high * mask, high * other], axis=0),
        jnp.concatenate([low * mask, low * other], axis=0),
    )


def pair_product(rows, high, low):
    right_high, right_low = block_diagonal(high, low)
    row_high, row_low = split(rows)
    dot = functools.partial(jnp.dot, preferred_element_type=jnp.float32)
    return dot(row_high, right_high) + (dot(row_low, right_high) + dot(row_high, right_low))


def stacked_product(rows, high, low):
    row_high, row_low = split(rows)
    product = jnp.dot(
        jnp.concatenate([row_high, row_low], axis=0),
        jnp.concatenate(block_diagonal(high, low), axis=1),
        preferred_element_type=jnp.float32,
    )
    count = rows.shape[0]
    return product[:count, :LANES] + (product[count:, :LANES] + product[:count, LANES:])


def fill_twins(field_tile, twin_ref, patch):
    swapped = pltpu.roll(field_tile, PN, 1)
    left = left_half(field_tile.shape)
    twin_ref[patch] = jnp.where(left, field_tile, swapped)
    twin_ref[patch + 1] = jnp.where(left, swapped, field_tile)


def side_by_side(first, second):
    return jnp.where(left_half(first.shape), first, second)


def scatter(force, step, targets):
    for slot in (2 * step, 2 * step + 1):
        for ref, patch, sign in targets(slot):
            ref[patch] = ref[patch] + force if sign > 0 else ref[patch] - force


def folded(total_ref, patch, other_ref):
    first = side_by_side(total_ref[patch], other_ref[patch])
    second = side_by_side(total_ref[patch + 1], other_ref[patch + 1])
    first = first + pltpu.roll(first, PN, 1)
    second = second + pltpu.roll(second, PN, 1)
    return jnp.where(left_half(first.shape), first, second)


def clear(total_ref):
    zero = jnp.zeros(total_ref.shape[1:], jnp.float32)
    for patch in range(total_ref.shape[0]):
        total_ref[patch] = zero


def prepare_kernel(
    field_hbm, stiff_hbm, contact_hbm, local_hbm, partner_hbm,
    field_ref, elastic_ref, stiff_high_ref, stiff_low_ref, contact_high_ref, contact_low_ref, local_ref, partner_ref,
    stiff_ref, contact_ref, sems, contact_sems, table_sems,
):
    chunk = stiff_ref.shape[1] // CHUNKS
    tiles = chunk // LANES
    copies = chunked((field_hbm, stiff_hbm), (field_ref, stiff_ref), sems, chunk)
    contact_copies = chunked((contact_hbm,), (contact_ref,), contact_sems, chunk)
    for group in copies + contact_copies:
        for copy in group:
            copy.start()
    slots = Slots((local_hbm, partner_hbm), (local_ref, partner_ref), table_sems)
    for place, group in enumerate(copies):
        for copy in group:
            copy.wait()
        for index in range(place * tiles, (place + 1) * tiles):
            high, low = split(tile(stiff_ref, index))
            put(stiff_high_ref, index, high)
            put(stiff_low_ref, index, low)
            put(elastic_ref, index, pair_product(tile(field_ref, index), high, low))
    for place, group in enumerate(contact_copies):
        for copy in group:
            copy.wait()
        for index in range(place * tiles, (place + 1) * tiles):
            high, low = split(tile(contact_ref, index))
            put(contact_high_ref, index, high)
            put(contact_low_ref, index, low)
    slots.wait()


def couple_kernel(
    count_ref, local_vmem, partner_vmem, field_ref, elastic_ref, halo_ref, high_ref, low_ref,
    total_ref, other_ref, gap_ref, force_ref, own_ref, spread_ref, even_ref, odd_ref,
    local_ref, partner_ref, table_sems, twin_ref,
):
    slots = Slots((local_vmem, partner_vmem), (local_ref, partner_ref), table_sems)
    patches = field_ref.shape[1] // PN
    clear(total_ref)
    clear(other_ref)
    for index in range(patches // 2):
        fill_twins(tile(field_ref, index), twin_ref, 2 * index)
    for index in range(NB // 2):
        fill_twins(tile(halo_ref, index), twin_ref, patches + 2 * index)
    slots.wait()

    def slot_gap(slot):
        return (twin_ref[slots.local[slot]] - twin_ref[slots.partner[slot]]) * live(count_ref, slot)

    def targets(slot):
        ref = (total_ref, other_ref)[slot % 2]
        return (ref, slots.local[slot], 1), (ref, slots.partner[slot], -1)

    for step in range(high_ref.shape[1] // LANES):
        gap = side_by_side(slot_gap(2 * step), slot_gap(2 * step + 1))
        force = stacked_product(gap, tile(high_ref, step), tile(low_ref, step))
        put(gap_ref, step, gap)
        put(force_ref, step, force)
        scatter(force, step, targets)
    even = lax.axis_index("dom") % 2 == 0
    for index in range(NB // 2):
        value = tile(elastic_ref, index) + folded(total_ref, 2 * index, other_ref)
        spread = folded(total_ref, patches + 2 * index, other_ref)
        put(own_ref, index, value)
        put(spread_ref, index, spread)
        put(even_ref, index, jnp.where(even, spread, value))
        put(odd_ref, index, jnp.where(even, value, spread))


def by_column(product, columns):
    total = product[:columns]
    for part in range(1, product.shape[0] // columns):
        total = total + product[part * columns : (part + 1) * columns]
    return total


class Sums:
    def __init__(self, columns):
        self.columns = columns
        self.values = {}

    def add(self, place, product):
        product = by_column(product, self.columns)
        self.values[place] = self.values[place] + product if place in self.values else product

    def load(self, ref):
        for place in range(SUMS):
            self.values[place] = ref[place * self.columns : (place + 1) * self.columns]

    def store(self, ref):
        for place in range(SUMS):
            zero = jnp.zeros((self.columns, LANES), jnp.float32)
            ref[place * self.columns : (place + 1) * self.columns] = self.values.get(place, zero)


def weights_of(weight_ref, index, rows):
    parts = weight_ref.shape[0]
    return jnp.concatenate(
        [
            jnp.broadcast_to(weight_ref[part : part + 1, index * LANES : (index + 1) * LANES], (rows // parts, LANES))
            for part in range(parts)
        ],
        axis=0,
    )


def add_energy(sums, trial_rows, field_part, field_force, image_part, image_force):
    rest = field_part - trial_rows * image_part
    sums.add(5, rest * (field_force - trial_rows * image_force))
    sums.add(6, rest * image_force)
    sums.add(7, image_part * image_force)


def lift_kernel(
    local_vmem, partner_vmem, field_ref, total_ref, other_ref, field_elastic_ref, stiff_high_ref, stiff_low_ref, weight_ref,
    image_ref, elastic_ref, near_ref, sums_ref, trial_ref,
    local_ref, partner_ref, table_sems, twin_ref, *, columns,
):
    slots = Slots((local_vmem, partner_vmem), (local_ref, partner_ref), table_sems)
    rows = field_ref.shape[0]
    patches = field_ref.shape[1] // PN
    lead = NB // 2
    sums = Sums(columns)
    for index in range(patches // 2):
        field_tile = tile(field_ref, index)
        weight_tile = weights_of(weight_ref, index, rows)
        sums.add(0, field_tile * field_tile)
        sums.add(8, weight_tile * field_tile)
        if index < lead:
            continue
        image_tile = tile(field_elastic_ref, index) + folded(total_ref, 2 * index, other_ref)
        put(image_ref, index - lead, image_tile)
        fill_twins(image_tile, twin_ref, 2 * index)
        product = pair_product(image_tile, tile(stiff_high_ref, index), tile(stiff_low_ref, index))
        put(elastic_ref, index - lead, product)
        sums.add(1, field_tile * image_tile)
        sums.add(4, image_tile * image_tile)
        sums.add(9, weight_tile * image_tile)
    across = jnp.sum(sums.values[1], axis=1, keepdims=True)
    square = jnp.sum(sums.values[4], axis=1, keepdims=True)
    some = square > 0.0
    trial = jnp.where(some, across / jnp.where(some, square, 1.0), 0.0)
    trial = jnp.broadcast_to(trial, (columns, LANES))
    trial_ref[...] = trial
    trial_rows = jnp.concatenate([trial] * (rows // columns), axis=0)
    for index in range(lead, patches // 2):
        field_tile, image_tile = tile(field_ref, index), tile(image_ref, index - lead)
        rest = field_tile - trial_rows * image_tile
        sums.add(2, rest * rest)
        sums.add(3, rest * image_tile)
        add_energy(
            sums, trial_rows, field_tile, tile(field_elastic_ref, index), image_tile, tile(elastic_ref, index - lead)
        )
    sums.store(sums_ref)
    twin_ref[patches] = jnp.zeros(twin_ref.shape[1:], jnp.float32)
    slots.wait()

    def inner(patch):
        return twin_ref[jnp.where((patch >= NB) & (patch < patches), patch, patches)]

    def inner_gap(slot):
        return inner(slots.local[slot]) - inner(slots.partner[slot])

    for step in range(near_ref.shape[1] // LANES):
        put(near_ref, step, side_by_side(inner_gap(2 * step), inner_gap(2 * step + 1)))


def energy_kernel(
    count_ref, local_vmem, partner_vmem, field_ref, field_elastic_ref, gap_ref, force_ref, own_ref, spread_ref,
    even_ref, odd_ref, near_ref, stiff_high_ref, stiff_low_ref, contact_high_ref, contact_low_ref, weight_ref,
    sums_ref, trial_ref,
    lead_ref, lead_elastic_ref, image_force_ref, moment_ref,
    local_ref, partner_ref, table_sems, twin_ref, *, columns,
):
    slots = Slots((local_vmem, partner_vmem), (local_ref, partner_ref), table_sems)
    rows = field_ref.shape[0]
    patches = field_ref.shape[1] // PN
    lead = NB // 2
    place, last = lax.axis_index("dom"), lax.axis_size("dom") - 1
    even = place % 2 == 0
    trial = trial_ref[...]
    trial_rows = jnp.concatenate([trial] * (rows // columns), axis=0)
    sums = Sums(columns)
    sums.load(sums_ref)
    for index in range(lead):
        first, second = tile(even_ref, index), tile(odd_ref, index)
        received = jnp.where(place > 0, jnp.where(even, second, first), 0.0)
        far_tile = jnp.where(place < last, jnp.where(even, first, second) + tile(spread_ref, index), 0.0)
        fill_twins(far_tile, twin_ref, NB + 2 * index)
        field_tile = tile(field_ref, index)
        image_tile = tile(own_ref, index) + received
        put(lead_ref, index, image_tile)
        fill_twins(image_tile, twin_ref, 2 * index)
        product = pair_product(image_tile, tile(stiff_high_ref, index), tile(stiff_low_ref, index))
        put(lead_elastic_ref, index, product)
        rest = field_tile - trial_rows * image_tile
        sums.add(1, field_tile * image_tile)
        sums.add(2, rest * rest)
        sums.add(3, rest * image_tile)
        sums.add(4, image_tile * image_tile)
        sums.add(9, weights_of(weight_ref, index, rows) * image_tile)
        add_energy(sums, trial_rows, field_tile, tile(field_elastic_ref, index), image_tile, product)
    twin_ref[2 * NB] = jnp.zeros(twin_ref.shape[1:], jnp.float32)
    slots.wait()

    def outer(patch):
        far = patch >= patches
        return twin_ref[jnp.where(far, patch - patches + NB, jnp.where(patch < NB, patch, 2 * NB))]

    def outer_gap(slot):
        return outer(slots.local[slot]) - outer(slots.partner[slot])

    for step in range(contact_high_ref.shape[1] // LANES):
        gap = tile(near_ref, step) + side_by_side(outer_gap(2 * step), outer_gap(2 * step + 1))
        lives = [jnp.full(gap.shape, live(count_ref, 2 * step + side), jnp.float32) for side in range(2)]
        gap = gap * side_by_side(*lives)
        force = stacked_product(gap, tile(contact_high_ref, step), tile(contact_low_ref, step))
        put(image_force_ref, step, force)
        add_energy(sums, trial_rows, tile(gap_ref, step), tile(force_ref, step), gap, force)
    lane = lax.broadcasted_iota(jnp.int32, (columns, LANES), 1)
    column = lax.broadcasted_iota(jnp.int32, (columns, LANES), 0)
    for half in range(2):
        spread_out = jnp.zeros((columns, LANES), jnp.float32)
        for number in range(half * 8, min(half * 8 + 8, SUMS + 1)):
            value = trial if number == SUMS else jnp.sum(sums.values[number], axis=1, keepdims=True)
            spread_out = jnp.where(lane == column + columns * (number % 8), value, spread_out)
        row = jnp.sum(spread_out, axis=0, keepdims=True)
        moment_ref[:, :, half * LANES : (half + 1) * LANES] = jnp.broadcast_to(
            row[None], (moment_ref.shape[0], 1, LANES)
        )


def settle_kernel(
    local_vmem, partner_vmem, force_ref, far_spread_ref, local_ref, partner_ref, table_sems, total_ref, other_ref, *, patches
):
    slots = Slots((local_vmem, partner_vmem), (local_ref, partner_ref), table_sems)
    clear(total_ref)
    clear(other_ref)
    slots.wait()

    def targets(slot):
        partner = slots.partner[slot]
        return (((total_ref, other_ref)[slot % 2], jnp.where(partner < patches, NB, partner - patches), -1),)

    for step in range(force_ref.shape[1] // LANES):
        scatter(tile(force_ref, step), step, targets)
    for index in range(NB // 2):
        put(far_spread_ref, index, folded(total_ref, 2 * index, other_ref))


def gather_kernel(
    local_vmem, partner_vmem, force_ref, lead_elastic_ref, elastic_ref, twice_ref,
    local_ref, partner_ref, table_sems, total_ref, other_ref,
):
    slots = Slots((local_vmem, partner_vmem), (local_ref, partner_ref), table_sems)
    patches = twice_ref.shape[1] // PN
    lead = NB // 2
    clear(total_ref)
    clear(other_ref)
    slots.wait()

    def targets(slot):
        partner = slots.partner[slot]
        ref = (total_ref, other_ref)[slot % 2]
        return (ref, slots.local[slot], 1), (ref, jnp.where(partner < patches, partner, patches), -1)

    for step in range(force_ref.shape[1] // LANES):
        scatter(tile(force_ref, step), step, targets)
    for index in range(patches // 2):
        product = tile(lead_elastic_ref, index) if index < lead else tile(elastic_ref, index - lead)
        put(twice_ref, index, product + folded(total_ref, 2 * index, other_ref))


def scale_kernel(moment_ref, scale_ref, gradient_ref, *, columns, groups):
    devices = moment_ref.shape[0]

    def moment(place):
        half = place // 8
        value = moment_ref[:, half * LANES : (half + 1) * LANES]
        shift = (LANES - columns * (place % 8)) % LANES
        if shift:
            value = pltpu.roll(value, shift, 1)
        return value.reshape(devices // 8, 8, LANES)

    def total(value):
        value = jnp.sum(value, axis=0)
        width = groups
        while width < 8:
            value = value + pltpu.roll(value, width, 0)
            width *= 2
        return value

    norm = total(moment(0))
    bend = total(moment(1))
    first_step = norm / bend
    change = first_step[None] - moment(SUMS)
    square = moment(4)
    mixed = moment(3)
    norm_next = total(moment(2) - 2.0 * change * mixed + change * change * square)
    drift = total(mixed - change * square)
    curve = total(moment(5) - 2.0 * change * moment(6) + change * change * moment(7))
    ratio = norm_next / norm
    bend_next = curve + 2.0 * ratio * drift + ratio * ratio * bend
    second_step = norm_next / bend_next
    on_field = first_step + second_step * (1.0 + ratio)
    on_image = -second_step * first_step
    gradient = on_field * total(moment(8)) + on_image * total(moment(9))
    gradient_ref[...] = gradient
    mine = lax.broadcasted_iota(jnp.int32, (8, LANES), 0) == lax.axis_index("col")
    diagonal = lax.broadcasted_iota(jnp.int32, (columns, LANES), 0) == lax.broadcasted_iota(
        jnp.int32, (columns, LANES), 1
    )
    for place, value in enumerate((on_field, on_image)):
        own = jnp.sum(jnp.where(mine, value, 0.0), axis=0, keepdims=True)
        own = jnp.sum(jnp.where(diagonal, own, 0.0), axis=1, keepdims=True)
        scale_ref[place * columns : (place + 1) * columns] = jnp.broadcast_to(own, (columns, LANES))


def own_step(gradient, columns, groups):
    lane = lax.broadcasted_iota(jnp.int32, (8, LANES), 1)
    row = lax.broadcasted_iota(jnp.int32, (8, LANES), 0)
    counted = jnp.where((lane < columns) & (row < groups), gradient * gradient, 0.0)
    square_total = jnp.sum(jnp.sum(counted, axis=1, keepdims=True), axis=0, keepdims=True)
    scaled = gradient / jnp.sqrt(square_total / (columns * groups) + 1e-06)
    return jnp.sum(jnp.where(row == lax.axis_index("col"), scaled, 0.0), axis=0, keepdims=True)[:, :columns]


def scale_rows(scale_ref, rows):
    columns = scale_ref.shape[0] // 2
    return (
        jnp.concatenate([scale_ref[:columns]] * (rows // columns), axis=0),
        jnp.concatenate([scale_ref[columns:]] * (rows // columns), axis=0),
    )


def last_kernel(
    scale_ref, gradient_ref, field_ref, image_ref, lead_ref, twice_ref, far_received_ref,
    solution_hbm, residual_hbm, step_hbm, solution_ref, residual_ref, step_ref, sems, step_sem, *, groups,
):
    field_rows, image_rows = scale_rows(scale_ref, field_ref.shape[0])
    chunk = field_ref.shape[1] // LAST_CHUNKS
    tiles = chunk // LANES
    copies = chunked((solution_ref, residual_ref), (solution_hbm, residual_hbm), sems, chunk)
    step_copy = pltpu.make_async_copy(step_ref, step_hbm, step_sem.at[0])
    for place, group in enumerate(copies):
        for index in range(place * tiles, (place + 1) * tiles):
            field_tile = tile(field_ref, index)
            image_tile = tile(lead_ref, index) if index < NB // 2 else tile(image_ref, index - NB // 2)
            twice_tile = tile(twice_ref, index)
            if index < NB // 2:
                twice_tile = twice_tile + tile(far_received_ref, index)
            put(solution_ref, index, field_rows * field_tile + image_rows * image_tile)
            put(residual_ref, index, field_tile - field_rows * image_tile - image_rows * twice_tile)
        for copy in group:
            copy.start()
        if place == 0:
            step_ref[...] = own_step(gradient_ref[...], scale_ref.shape[0] // 2, groups)
            step_copy.start()
    step_copy.wait()
    for group in copies:
        for copy in group:
            copy.wait()


def shards(right_side, stiffness, contact, pair_local, pair_partner, pair_count, objective_weight):
    components, columns, nodes = right_side.shape
    rows = components * columns
    patches = nodes // PN
    groups = lax.axis_size("col")
    chain_length = lax.axis_size("dom")
    devices = chain_length * groups
    f32 = jnp.float32
    width = NB * PN
    call = functools.partial(
        pl.pallas_call, compiler_params=pltpu.CompilerParams(vmem_limit_bytes=8 * 1024 * 1024)
    )
    shape = jax.ShapeDtypeStruct
    wide = shape((rows, nodes), f32)
    narrow = shape((rows, width), f32)
    parts = [shape(block.shape, jnp.bfloat16) for block in (stiffness, stiffness, contact, contact)]

    def in_hbm(value):
        return pltpu.with_memory_space_constraint(value, pltpu.HBM)

    field_hbm = in_hbm(right_side.reshape(rows, nodes))
    pairs = (in_hbm(pair_local), in_hbm(pair_partner))
    slots = shape((rows, contact.shape[1]), f32)

    def scratch(count, copies=1):
        return [
            pltpu.SMEM(pair_local.shape, jnp.int32),
            pltpu.SMEM(pair_partner.shape, jnp.int32),
            pltpu.SemaphoreType.DMA((2,)),
        ] + [pltpu.VMEM((count, rows, LANES), f32)] * copies

    halo = shifted(right_side[:, :, :width], "dom", -1).reshape(rows, width)
    field, field_elastic, stiff_high, stiff_low, contact_high, contact_low, *tables = call(
        prepare_kernel,
        out_shape=(wide, wide, *parts, *(shape(pair.shape, jnp.int32) for pair in pairs)),
        in_specs=[HBM] * 5,
        out_specs=(VMEM,) * 8,
        scratch_shapes=[
            pltpu.VMEM(stiffness.shape, f32),
            pltpu.VMEM(contact.shape, f32),
            pltpu.SemaphoreType.DMA((2 * CHUNKS,)),
            pltpu.SemaphoreType.DMA((CHUNKS,)),
            pltpu.SemaphoreType.DMA((2,)),
        ],
        name="prepare",
    )(field_hbm, in_hbm(stiffness), in_hbm(contact), *pairs)
    total, other, gap, force, own, spread, even, odd = call(
        couple_kernel,
        out_shape=(*[shape((patches + NB, rows, LANES), f32)] * 2, slots, slots, narrow, narrow, narrow, narrow),
        in_specs=[SMEM] + [VMEM] * 7,
        out_specs=(VMEM,) * 8,
        scratch_shapes=scratch(patches + NB),
        name="couple",
    )(pair_count, *tables, field, field_elastic, halo, contact_high, contact_low)
    even = swapped(even, False)
    odd = swapped(odd, True)
    tail = shape((rows, nodes - width), f32)
    image, elastic, near, sums, trial = call(
        functools.partial(lift_kernel, columns=columns),
        out_shape=(tail, tail, slots, shape((SUMS * columns, LANES), f32), shape((columns, LANES), f32)),
        in_specs=[VMEM] * 9,
        out_specs=(VMEM,) * 5,
        scratch_shapes=scratch(patches + 1),
        name="lift",
    )(*tables, field, total, other, field_elastic, stiff_high, stiff_low, objective_weight)
    lead, lead_elastic, image_force, moments = call(
        functools.partial(energy_kernel, columns=columns),
        out_shape=(narrow, narrow, slots, shape((devices, 1, MOMENT_LANES), f32)),
        in_specs=[SMEM] + [VMEM] * 18,
        out_specs=(VMEM,) * 4,
        scratch_shapes=scratch(2 * NB + 1),
        name="energy",
    )(
        pair_count, *tables, field, field_elastic, gap, force, own, spread, even, odd, near,
        stiff_high, stiff_low, contact_high, contact_low, objective_weight, sums, trial,
    )
    gathered = lax.all_to_all(moments, ("dom", "col"), 0, 0, tiled=True).reshape(devices, MOMENT_LANES)
    far_spread = call(
        functools.partial(settle_kernel, patches=patches),
        out_shape=narrow,
        in_specs=[VMEM] * 3,
        out_specs=VMEM,
        scratch_shapes=scratch(NB + 1, 2),
        cost_estimate=pl.CostEstimate(flops=10**9, bytes_accessed=rows * nodes * 4, transcendentals=0),
        name="settle",
    )(*tables, image_force)
    far_received = shifted(far_spread, "dom", 1)
    twice = call(
        gather_kernel,
        out_shape=wide,
        in_specs=[VMEM] * 5,
        out_specs=VMEM,
        scratch_shapes=scratch(patches + 1, 2),
        cost_estimate=pl.CostEstimate(flops=10**9, bytes_accessed=3 * rows * nodes * 4, transcendentals=0),
        name="gather",
    )(*tables, image_force, lead_elastic, elastic)
    scales, gradient = call(
        functools.partial(scale_kernel, columns=columns, groups=groups),
        out_shape=(shape((2 * columns, LANES), f32), shape((8, LANES), f32)),
        in_specs=[VMEM],
        out_specs=(VMEM,) * 2,
        cost_estimate=pl.CostEstimate(flops=10**9, bytes_accessed=devices * MOMENT_LANES * 4, transcendentals=0),
        name="scale",
    )(gathered)
    solution_field, residual, step = call(
        functools.partial(last_kernel, groups=groups),
        out_shape=(wide, wide, shape((1, columns), f32)),
        in_specs=[VMEM] * 7,
        out_specs=(HBM,) * 3,
        scratch_shapes=[pltpu.VMEM((rows, nodes), f32)] * 2
        + [
            pltpu.VMEM((1, columns), f32),
            pltpu.SemaphoreType.DMA((2 * LAST_CHUNKS,)),
            pltpu.SemaphoreType.DMA((1,)),
        ],
        name="last",
    )(scales, gradient, field, image, lead, twice, far_received)
    return (
        solution_field.reshape(right_side.shape),
        residual.reshape(right_side.shape),
        step.reshape(columns),
    )


def solution(mesh):
    placed = (
        P(None, "col", "dom"),
        P(None, "dom"),
        P(None, "dom"),
        P("dom"),
        P("dom"),
        P("dom"),
        P(None, "dom"),
    )
    return jax.shard_map(
        shards,
        mesh=mesh,
        in_specs=placed,
        out_specs=(P(None, "col", "dom"), P(None, "col", "dom"), P("col")),
        check_vma=False,
    )
```

```python
import functools

import jax
import jax.numpy as jnp
from jax import lax
from jax.experimental import pallas as pl
from jax.experimental.pallas import tpu as pltpu
from jax.sharding import PartitionSpec as P

PN = 64
NB = 8
LANES = 128
SMEM = pl.BlockSpec(memory_space=pltpu.SMEM)
MOMENT_LANES = 256
VMEM = pl.BlockSpec(memory_space=pltpu.VMEM)
HBM = pl.BlockSpec(memory_space=pltpu.HBM)
SUMS = 10
CHUNKS = 4
LAST_CHUNKS = 4


def shifted(value, axis, by):
    count = lax.axis_size(axis)
    pairs = [(i, i + by) for i in range(count) if 0 <= i + by < count]
    return lax.ppermute(value, axis, pairs)


def swapped(value, odd):
    count, groups = lax.axis_size("dom"), lax.axis_size("col")
    pairs = []
    for place in range(count):
        partner = place + 1 if (place % 2 == 1) == odd else place - 1
        for column in range(groups):
            if 0 <= partner < count:
                pairs.append((place * groups + column, partner * groups + column))
            else:
                beside = column ^ 1 if column ^ 1 < groups else column
                pairs.append((place * groups + column, place * groups + beside))
    return lax.ppermute(value, ("dom", "col"), pairs)


def left_half(shape):
    return lax.broadcasted_iota(jnp.int32, shape, len(shape) - 1) < PN


def split(value):
    high = value.astype(jnp.bfloat16)
    low = (value - high.astype(jnp.float32)).astype(jnp.bfloat16)
    return high, low


def tile(ref, index):
    return ref[:, index * LANES : (index + 1) * LANES]


def put(ref, index, value):
    ref[:, index * LANES : (index + 1) * LANES] = value


class Slots:
    def __init__(self, sources, targets, sems):
        self.local, self.partner = targets
        self.copies = [
            pltpu.make_async_copy(source, target, sems.at[place])
            for place, (source, target) in enumerate(zip(sources, targets))
        ]
        for copy in self.copies:
            copy.start()

    def wait(self):
        for copy in self.copies:
            copy.wait()


def chunked(sources, targets, sems, chunk):
    copies = []
    for start in range(0, targets[0].shape[1], chunk):
        lanes = pl.ds(start, chunk)
        group = []
        for source, target in zip(sources, targets):
            group.append(
                pltpu.make_async_copy(source.at[:, lanes], target.at[:, lanes], sems.at[len(copies) * len(targets) + len(group)])
            )
        copies.append(group)
    return copies


def block_diagonal(high, low):
    mask = left_half((PN, LANES)).astype(jnp.bfloat16)
    other = (1 - left_half((PN, LANES)).astype(jnp.int32)).astype(jnp.bfloat16)
    return (
        jnp.concatenate([high * mask, high * other], axis=0),
        jnp.concatenate([low * mask, low * other], axis=0),
    )


def pair_product(rows, high, low):
    right_high, right_low = block_diagonal(high, low)
    row_high, row_low = split(rows)
    dot = functools.partial(jnp.dot, preferred_element_type=jnp.float32)
    return dot(row_high, right_high) + (dot(row_low, right_high) + dot(row_high, right_low))


def stacked_product(rows, high, low):
    row_high, row_low = split(rows)
    product = jnp.dot(
        jnp.concatenate([row_high, row_low], axis=0),
        jnp.concatenate(block_diagonal(high, low), axis=1),
        preferred_element_type=jnp.float32,
    )
    count = rows.shape[0]
    return product[:count, :LANES] + (product[count:, :LANES] + product[:count, LANES:])


def fill_twins(field_tile, twin_ref, patch):
    swapped = pltpu.roll(field_tile, PN, 1)
    left = left_half(field_tile.shape)
    twin_ref[patch] = jnp.where(left, field_tile, swapped)
    twin_ref[patch + 1] = jnp.where(left, swapped, field_tile)


def side_by_side(first, second):
    return jnp.where(left_half(first.shape), first, second)


def scatter(force, step, targets):
    for slot in (2 * step, 2 * step + 1):
        for ref, patch, sign in targets(slot):
            ref[patch] = ref[patch] + force if sign > 0 else ref[patch] - force


def folded(total_ref, patch, other_ref):
    first = side_by_side(total_ref[patch], other_ref[patch])
    second = side_by_side(total_ref[patch + 1], other_ref[patch + 1])
    first = first + pltpu.roll(first, PN, 1)
    second = second + pltpu.roll(second, PN, 1)
    return jnp.where(left_half(first.shape), first, second)


def clear(total_ref):
    zero = jnp.zeros(total_ref.shape[1:], jnp.float32)
    for patch in range(total_ref.shape[0]):
        total_ref[patch] = zero


def prepare_kernel(
    field_hbm, stiff_hbm, contact_hbm, local_hbm, partner_hbm,
    field_ref, elastic_ref, stiff_high_ref, stiff_low_ref, contact_high_ref, contact_low_ref, local_ref, partner_ref,
    stiff_ref, contact_ref, sems, contact_sems, table_sems,
):
    chunk = stiff_ref.shape[1] // CHUNKS
    tiles = chunk // LANES
    copies = chunked((field_hbm, stiff_hbm), (field_ref, stiff_ref), sems, chunk)
    contact_copies = chunked((contact_hbm,), (contact_ref,), contact_sems, chunk)
    for group in copies + contact_copies:
        for copy in group:
            copy.start()
    slots = Slots((local_hbm, partner_hbm), (local_ref, partner_ref), table_sems)
    for place, group in enumerate(copies):
        for copy in group:
            copy.wait()
        for index in range(place * tiles, (place + 1) * tiles):
            high, low = split(tile(stiff_ref, index))
            put(stiff_high_ref, index, high)
            put(stiff_low_ref, index, low)
            put(elastic_ref, index, pair_product(tile(field_ref, index), high, low))
    for place, group in enumerate(contact_copies):
        for copy in group:
            copy.wait()
        for index in range(place * tiles, (place + 1) * tiles):
            high, low = split(tile(contact_ref, index))
            put(contact_high_ref, index, high)
            put(contact_low_ref, index, low)
    slots.wait()


def couple_kernel(
    count_ref, local_vmem, partner_vmem, field_ref, elastic_ref, halo_ref, high_ref, low_ref,
    total_ref, other_ref, gap_ref, force_ref, own_ref, spread_ref, even_ref, odd_ref,
    local_ref, partner_ref, table_sems, twin_ref,
):
    slots = Slots((local_vmem, partner_vmem), (local_ref, partner_ref), table_sems)
    patches = field_ref.shape[1] // PN
    clear(total_ref)
    clear(other_ref)
    for index in range(patches // 2):
        fill_twins(tile(field_ref, index), twin_ref, 2 * index)
    for index in range(NB // 2):
        fill_twins(tile(halo_ref, index), twin_ref, patches + 2 * index)
    slots.wait()

    def slot_gap(slot):
        patch = slots.local[slot]
        partner = jnp.where(slot < count_ref[0], slots.partner[slot], patch)
        return twin_ref[patch] - twin_ref[partner]

    def targets(slot):
        ref = (total_ref, other_ref)[slot % 2]
        return (ref, slots.local[slot], 1), (ref, slots.partner[slot], -1)

    for step in range(high_ref.shape[1] // LANES):
        gap = side_by_side(slot_gap(2 * step), slot_gap(2 * step + 1))
        force = stacked_product(gap, tile(high_ref, step), tile(low_ref, step))
        put(gap_ref, step, gap)
        put(force_ref, step, force)
        scatter(force, step, targets)
    even = lax.axis_index("dom") % 2 == 0
    for index in range(NB // 2):
        value = tile(elastic_ref, index) + folded(total_ref, 2 * index, other_ref)
        spread = folded(total_ref, patches + 2 * index, other_ref)
        put(own_ref, index, value)
        put(spread_ref, index, spread)
        put(even_ref, index, jnp.where(even, spread, value))
        put(odd_ref, index, jnp.where(even, value, spread))


def by_column(product, columns):
    total = product[:columns]
    for part in range(1, product.shape[0] // columns):
        total = total + product[part * columns : (part + 1) * columns]
    return total


class Sums:
    def __init__(self, columns):
        self.columns = columns
        self.values = {}

    def add(self, place, product):
        product = by_column(product, self.columns)
        self.values[place] = self.values[place] + product if place in self.values else product

    def load(self, ref):
        for place in range(SUMS):
            self.values[place] = ref[place * self.columns : (place + 1) * self.columns]

    def store(self, ref):
        for place in range(SUMS):
            zero = jnp.zeros((self.columns, LANES), jnp.float32)
            ref[place * self.columns : (place + 1) * self.columns] = self.values.get(place, zero)


def weights_of(weight_ref, index, rows):
    parts = weight_ref.shape[0]
    return jnp.concatenate(
        [
            jnp.broadcast_to(weight_ref[part : part + 1, index * LANES : (index + 1) * LANES], (rows // parts, LANES))
            for part in range(parts)
        ],
        axis=0,
    )


def add_energy(sums, trial_rows, field_part, field_force, image_part, image_force):
    rest = field_part - trial_rows * image_part
    sums.add(5, rest * (field_force - trial_rows * image_force))
    sums.add(6, rest * image_force)
    sums.add(7, image_part * image_force)


def lift_kernel(
    count_ref, local_vmem, partner_vmem, field_ref, total_ref, other_ref, field_elastic_ref, stiff_high_ref, stiff_low_ref, weight_ref,
    image_ref, elastic_ref, near_ref, sums_ref, trial_ref,
    local_ref, partner_ref, table_sems, twin_ref, *, columns,
):
    slots = Slots((local_vmem, partner_vmem), (local_ref, partner_ref), table_sems)
    rows = field_ref.shape[0]
    patches = field_ref.shape[1] // PN
    lead = NB // 2
    sums = Sums(columns)
    for index in range(patches // 2):
        field_tile = tile(field_ref, index)
        weight_tile = weights_of(weight_ref, index, rows)
        sums.add(0, field_tile * field_tile)
        sums.add(8, weight_tile * field_tile)
        if index < lead:
            continue
        image_tile = tile(field_elastic_ref, index) + folded(total_ref, 2 * index, other_ref)
        put(image_ref, index - lead, image_tile)
        fill_twins(image_tile, twin_ref, 2 * index)
        product = pair_product(image_tile, tile(stiff_high_ref, index), tile(stiff_low_ref, index))
        put(elastic_ref, index - lead, product)
        sums.add(1, field_tile * image_tile)
        sums.add(4, image_tile * image_tile)
        sums.add(9, weight_tile * image_tile)
    across = jnp.sum(sums.values[1], axis=1, keepdims=True)
    square = jnp.sum(sums.values[4], axis=1, keepdims=True)
    some = square > 0.0
    trial = jnp.where(some, across / jnp.where(some, square, 1.0), 0.0)
    trial = jnp.broadcast_to(trial, (columns, LANES))
    trial_ref[...] = trial
    trial_rows = jnp.concatenate([trial] * (rows // columns), axis=0)
    for index in range(lead, patches // 2):
        field_tile, image_tile = tile(field_ref, index), tile(image_ref, index - lead)
        rest = field_tile - trial_rows * image_tile
        sums.add(2, rest * rest)
        sums.add(3, rest * image_tile)
        add_energy(
            sums, trial_rows, field_tile, tile(field_elastic_ref, index), image_tile, tile(elastic_ref, index - lead)
        )
    sums.store(sums_ref)
    twin_ref[patches] = jnp.zeros(twin_ref.shape[1:], jnp.float32)
    slots.wait()

    def inner(slot, patch):
        return twin_ref[jnp.where((slot < count_ref[0]) & (patch >= NB) & (patch < patches), patch, patches)]

    def inner_gap(slot):
        return inner(slot, slots.local[slot]) - inner(slot, slots.partner[slot])

    for step in range(near_ref.shape[1] // LANES):
        put(near_ref, step, side_by_side(inner_gap(2 * step), inner_gap(2 * step + 1)))


def energy_kernel(
    count_ref, local_vmem, partner_vmem, field_ref, field_elastic_ref, gap_ref, force_ref, own_ref, spread_ref,
    even_ref, odd_ref, near_ref, stiff_high_ref, stiff_low_ref, contact_high_ref, contact_low_ref, weight_ref,
    sums_ref, trial_ref,
    lead_ref, lead_elastic_ref, image_force_ref, moment_ref,
    local_ref, partner_ref, table_sems, twin_ref, *, columns,
):
    slots = Slots((local_vmem, partner_vmem), (local_ref, partner_ref), table_sems)
    rows = field_ref.shape[0]
    patches = field_ref.shape[1] // PN
    lead = NB // 2
    place, last = lax.axis_index("dom"), lax.axis_size("dom") - 1
    even = place % 2 == 0
    trial = trial_ref[...]
    trial_rows = jnp.concatenate([trial] * (rows // columns), axis=0)
    sums = Sums(columns)
    sums.load(sums_ref)
    for index in range(lead):
        first, second = tile(even_ref, index), tile(odd_ref, index)
        received = jnp.where(place > 0, jnp.where(even, second, first), 0.0)
        far_tile = jnp.where(place < last, jnp.where(even, first, second) + tile(spread_ref, index), 0.0)
        fill_twins(far_tile, twin_ref, NB + 2 * index)
        field_tile = tile(field_ref, index)
        image_tile = tile(own_ref, index) + received
        put(lead_ref, index, image_tile)
        fill_twins(image_tile, twin_ref, 2 * index)
        product = pair_product(image_tile, tile(stiff_high_ref, index), tile(stiff_low_ref, index))
        put(lead_elastic_ref, index, product)
        rest = field_tile - trial_rows * image_tile
        sums.add(1, field_tile * image_tile)
        sums.add(2, rest * rest)
        sums.add(3, rest * image_tile)
        sums.add(4, image_tile * image_tile)
        sums.add(9, weights_of(weight_ref, index, rows) * image_tile)
        add_energy(sums, trial_rows, field_tile, tile(field_elastic_ref, index), image_tile, product)
    twin_ref[2 * NB] = jnp.zeros(twin_ref.shape[1:], jnp.float32)
    slots.wait()

    def outer(slot, patch):
        here = jnp.where(patch >= patches, patch - patches + NB, jnp.where(patch < NB, patch, 2 * NB))
        return twin_ref[jnp.where(slot < count_ref[0], here, 2 * NB)]

    def outer_gap(slot):
        return outer(slot, slots.local[slot]) - outer(slot, slots.partner[slot])

    for step in range(contact_high_ref.shape[1] // LANES):
        gap = tile(near_ref, step) + side_by_side(outer_gap(2 * step), outer_gap(2 * step + 1))
        force = stacked_product(gap, tile(contact_high_ref, step), tile(contact_low_ref, step))
        put(image_force_ref, step, force)
        add_energy(sums, trial_rows, tile(gap_ref, step), tile(force_ref, step), gap, force)
    lane = lax.broadcasted_iota(jnp.int32, (columns, LANES), 1)
    column = lax.broadcasted_iota(jnp.int32, (columns, LANES), 0)
    for half in range(2):
        spread_out = jnp.zeros((columns, LANES), jnp.float32)
        for number in range(half * 8, min(half * 8 + 8, SUMS + 1)):
            value = trial if number == SUMS else jnp.sum(sums.values[number], axis=1, keepdims=True)
            spread_out = jnp.where(lane == column + columns * (number % 8), value, spread_out)
        row = jnp.sum(spread_out, axis=0, keepdims=True)
        moment_ref[:, :, half * LANES : (half + 1) * LANES] = jnp.broadcast_to(
            row[None], (moment_ref.shape[0], 1, LANES)
        )


def settle_kernel(
    local_vmem, partner_vmem, force_ref, far_spread_ref, local_ref, partner_ref, table_sems, total_ref, other_ref, *, patches
):
    slots = Slots((local_vmem, partner_vmem), (local_ref, partner_ref), table_sems)
    clear(total_ref)
    clear(other_ref)
    slots.wait()

    def targets(slot):
        partner = slots.partner[slot]
        return (((total_ref, other_ref)[slot % 2], jnp.where(partner < patches, NB, partner - patches), -1),)

    for step in range(force_ref.shape[1] // LANES):
        scatter(tile(force_ref, step), step, targets)
    for index in range(NB // 2):
        put(far_spread_ref, index, folded(total_ref, 2 * index, other_ref))


def gather_kernel(
    local_vmem, partner_vmem, force_ref, lead_elastic_ref, elastic_ref, twice_ref,
    local_ref, partner_ref, table_sems, total_ref, other_ref,
):
    slots = Slots((local_vmem, partner_vmem), (local_ref, partner_ref), table_sems)
    patches = twice_ref.shape[1] // PN
    lead = NB // 2
    clear(total_ref)
    clear(other_ref)
    slots.wait()

    def targets(slot):
        partner = slots.partner[slot]
        ref = (total_ref, other_ref)[slot % 2]
        return (ref, slots.local[slot], 1), (ref, jnp.where(partner < patches, partner, patches), -1)

    for step in range(force_ref.shape[1] // LANES):
        scatter(tile(force_ref, step), step, targets)
    for index in range(patches // 2):
        product = tile(lead_elastic_ref, index) if index < lead else tile(elastic_ref, index - lead)
        put(twice_ref, index, product + folded(total_ref, 2 * index, other_ref))


def scale_kernel(moment_ref, scale_ref, gradient_ref, *, columns, groups):
    devices = moment_ref.shape[0]

    def moment(place):
        half = place // 8
        value = moment_ref[:, half * LANES : (half + 1) * LANES]
        shift = (LANES - columns * (place % 8)) % LANES
        if shift:
            value = pltpu.roll(value, shift, 1)
        return value.reshape(devices // 8, 8, LANES)

    def total(value):
        value = jnp.sum(value, axis=0)
        width = groups
        while width < 8:
            value = value + pltpu.roll(value, width, 0)
            width *= 2
        return value

    norm = total(moment(0))
    bend = total(moment(1))
    first_step = norm / bend
    change = first_step[None] - moment(SUMS)
    square = moment(4)
    mixed = moment(3)
    norm_next = total(moment(2) - 2.0 * change * mixed + change * change * square)
    drift = total(mixed - change * square)
    curve = total(moment(5) - 2.0 * change * moment(6) + change * change * moment(7))
    ratio = norm_next / norm
    bend_next = curve + 2.0 * ratio * drift + ratio * ratio * bend
    second_step = norm_next / bend_next
    on_field = first_step + second_step * (1.0 + ratio)
    on_image = -second_step * first_step
    gradient = on_field * total(moment(8)) + on_image * total(moment(9))
    gradient_ref[...] = gradient
    mine = lax.broadcasted_iota(jnp.int32, (8, LANES), 0) == lax.axis_index("col")
    diagonal = lax.broadcasted_iota(jnp.int32, (columns, LANES), 0) == lax.broadcasted_iota(
        jnp.int32, (columns, LANES), 1
    )
    for place, value in enumerate((on_field, on_image)):
        own = jnp.sum(jnp.where(mine, value, 0.0), axis=0, keepdims=True)
        own = jnp.sum(jnp.where(diagonal, own, 0.0), axis=1, keepdims=True)
        scale_ref[place * columns : (place + 1) * columns] = jnp.broadcast_to(own, (columns, LANES))


def own_step(gradient, columns, groups):
    lane = lax.broadcasted_iota(jnp.int32, (8, LANES), 1)
    row = lax.broadcasted_iota(jnp.int32, (8, LANES), 0)
    counted = jnp.where((lane < columns) & (row < groups), gradient * gradient, 0.0)
    square_total = jnp.sum(jnp.sum(counted, axis=1, keepdims=True), axis=0, keepdims=True)
    scaled = gradient / jnp.sqrt(square_total / (columns * groups) + 1e-06)
    return jnp.sum(jnp.where(row == lax.axis_index("col"), scaled, 0.0), axis=0, keepdims=True)[:, :columns]


def scale_rows(scale_ref, rows):
    columns = scale_ref.shape[0] // 2
    return (
        jnp.concatenate([scale_ref[:columns]] * (rows // columns), axis=0),
        jnp.concatenate([scale_ref[columns:]] * (rows // columns), axis=0),
    )


def last_kernel(
    scale_ref, gradient_ref, field_ref, image_ref, lead_ref, twice_ref, far_received_ref,
    solution_hbm, residual_hbm, step_hbm, solution_ref, residual_ref, step_ref, sems, step_sem, *, groups,
):
    field_rows, image_rows = scale_rows(scale_ref, field_ref.shape[0])
    chunk = field_ref.shape[1] // LAST_CHUNKS
    tiles = chunk // LANES
    copies = chunked((solution_ref, residual_ref), (solution_hbm, residual_hbm), sems, chunk)
    step_copy = pltpu.make_async_copy(step_ref, step_hbm, step_sem.at[0])
    for place, group in enumerate(copies):
        for index in range(place * tiles, (place + 1) * tiles):
            field_tile = tile(field_ref, index)
            image_tile = tile(lead_ref, index) if index < NB // 2 else tile(image_ref, index - NB // 2)
            twice_tile = tile(twice_ref, index)
            if index < NB // 2:
                twice_tile = twice_tile + tile(far_received_ref, index)
            put(solution_ref, index, field_rows * field_tile + image_rows * image_tile)
            put(residual_ref, index, field_tile - field_rows * image_tile - image_rows * twice_tile)
        for copy in group:
            copy.start()
        if place == 0:
            step_ref[...] = own_step(gradient_ref[...], scale_ref.shape[0] // 2, groups)
            step_copy.start()
    step_copy.wait()
    for group in copies:
        for copy in group:
            copy.wait()


def shards(right_side, stiffness, contact, pair_local, pair_partner, pair_count, objective_weight):
    components, columns, nodes = right_side.shape
    rows = components * columns
    patches = nodes // PN
    groups = lax.axis_size("col")
    chain_length = lax.axis_size("dom")
    devices = chain_length * groups
    f32 = jnp.float32
    width = NB * PN
    call = functools.partial(
        pl.pallas_call, compiler_params=pltpu.CompilerParams(vmem_limit_bytes=8 * 1024 * 1024)
    )
    shape = jax.ShapeDtypeStruct
    wide = shape((rows, nodes), f32)
    narrow = shape((rows, width), f32)
    parts = [shape(block.shape, jnp.bfloat16) for block in (stiffness, stiffness, contact, contact)]

    def in_hbm(value):
        return pltpu.with_memory_space_constraint(value, pltpu.HBM)

    field_hbm = in_hbm(right_side.reshape(rows, nodes))
    pairs = (in_hbm(pair_local), in_hbm(pair_partner))
    slots = shape((rows, contact.shape[1]), f32)

    def scratch(count, copies=1):
        return [
            pltpu.SMEM(pair_local.shape, jnp.int32),
            pltpu.SMEM(pair_partner.shape, jnp.int32),
            pltpu.SemaphoreType.DMA((2,)),
        ] + [pltpu.VMEM((count, rows, LANES), f32)] * copies

    halo = shifted(right_side[:, :, :width], "dom", -1).reshape(rows, width)
    field, field_elastic, stiff_high, stiff_low, contact_high, contact_low, *tables = call(
        prepare_kernel,
        out_shape=(wide, wide, *parts, *(shape(pair.shape, jnp.int32) for pair in pairs)),
        in_specs=[HBM] * 5,
        out_specs=(VMEM,) * 8,
        scratch_shapes=[
            pltpu.VMEM(stiffness.shape, f32),
            pltpu.VMEM(contact.shape, f32),
            pltpu.SemaphoreType.DMA((2 * CHUNKS,)),
            pltpu.SemaphoreType.DMA((CHUNKS,)),
            pltpu.SemaphoreType.DMA((2,)),
        ],
        name="prepare",
    )(field_hbm, in_hbm(stiffness), in_hbm(contact), *pairs)
    total, other, gap, force, own, spread, even, odd = call(
        couple_kernel,
        out_shape=(*[shape((patches + NB, rows, LANES), f32)] * 2, slots, slots, narrow, narrow, narrow, narrow),
        in_specs=[SMEM] + [VMEM] * 7,
        out_specs=(VMEM,) * 8,
        scratch_shapes=scratch(patches + NB),
        name="couple",
    )(pair_count, *tables, field, field_elastic, halo, contact_high, contact_low)
    even = swapped(even, False)
    odd = swapped(odd, True)
    tail = shape((rows, nodes - width), f32)
    image, elastic, near, sums, trial = call(
        functools.partial(lift_kernel, columns=columns),
        out_shape=(tail, tail, slots, shape((SUMS * columns, LANES), f32), shape((columns, LANES), f32)),
        in_specs=[SMEM] + [VMEM] * 9,
        out_specs=(VMEM,) * 5,
        scratch_shapes=scratch(patches + 1),
        name="lift",
    )(pair_count, *tables, field, total, other, field_elastic, stiff_high, stiff_low, objective_weight)
    lead, lead_elastic, image_force, moments = call(
        functools.partial(energy_kernel, columns=columns),
        out_shape=(narrow, narrow, slots, shape((devices, 1, MOMENT_LANES), f32)),
        in_specs=[SMEM] + [VMEM] * 18,
        out_specs=(VMEM,) * 4,
        scratch_shapes=scratch(2 * NB + 1),
        name="energy",
    )(
        pair_count, *tables, field, field_elastic, gap, force, own, spread, even, odd, near,
        stiff_high, stiff_low, contact_high, contact_low, objective_weight, sums, trial,
    )
    gathered = lax.all_to_all(moments, ("dom", "col"), 0, 0, tiled=True).reshape(devices, MOMENT_LANES)
    far_spread = call(
        functools.partial(settle_kernel, patches=patches),
        out_shape=narrow,
        in_specs=[VMEM] * 3,
        out_specs=VMEM,
        scratch_shapes=scratch(NB + 1, 2),
        cost_estimate=pl.CostEstimate(flops=10**9, bytes_accessed=rows * nodes * 4, transcendentals=0),
        name="settle",
    )(*tables, image_force)
    far_received = shifted(far_spread, "dom", 1)
    twice = call(
        gather_kernel,
        out_shape=wide,
        in_specs=[VMEM] * 5,
        out_specs=VMEM,
        scratch_shapes=scratch(patches + 1, 2),
        cost_estimate=pl.CostEstimate(flops=10**9, bytes_accessed=3 * rows * nodes * 4, transcendentals=0),
        name="gather",
    )(*tables, image_force, lead_elastic, elastic)
    scales, gradient = call(
        functools.partial(scale_kernel, columns=columns, groups=groups),
        out_shape=(shape((2 * columns, LANES), f32), shape((8, LANES), f32)),
        in_specs=[VMEM],
        out_specs=(VMEM,) * 2,
        cost_estimate=pl.CostEstimate(flops=10**9, bytes_accessed=devices * MOMENT_LANES * 4, transcendentals=0),
        name="scale",
    )(gathered)
    solution_field, residual, step = call(
        functools.partial(last_kernel, groups=groups),
        out_shape=(wide, wide, shape((1, columns), f32)),
        in_specs=[VMEM] * 7,
        out_specs=(HBM,) * 3,
        scratch_shapes=[pltpu.VMEM((rows, nodes), f32)] * 2
        + [
            pltpu.VMEM((1, columns), f32),
            pltpu.SemaphoreType.DMA((2 * LAST_CHUNKS,)),
            pltpu.SemaphoreType.DMA((1,)),
        ],
        name="last",
    )(scales, gradient, field, image, lead, twice, far_received)
    return (
        solution_field.reshape(right_side.shape),
        residual.reshape(right_side.shape),
        step.reshape(columns),
    )


def solution(mesh):
    placed = (
        P(None, "col", "dom"),
        P(None, "dom"),
        P(None, "dom"),
        P("dom"),
        P("dom"),
        P("dom"),
        P(None, "dom"),
    )
    return jax.shard_map(
        shards,
        mesh=mesh,
        in_specs=placed,
        out_specs=(P(None, "col", "dom"), P(None, "col", "dom"), P("col")),
        check_vma=False,
    )
```

```python
import functools

import jax
import jax.numpy as jnp
from jax import lax
from jax.experimental import pallas as pl
from jax.experimental.pallas import tpu as pltpu
from jax.sharding import PartitionSpec as P

PN = 64
NB = 8
LANES = 128
SMEM = pl.BlockSpec(memory_space=pltpu.SMEM)
MOMENT_LANES = 256
VMEM = pl.BlockSpec(memory_space=pltpu.VMEM)
HBM = pl.BlockSpec(memory_space=pltpu.HBM)
SUMS = 10
CHUNKS = 4
LAST_CHUNKS = 4


def shifted(value, axis, by):
    count = lax.axis_size(axis)
    pairs = [(i, i + by) for i in range(count) if 0 <= i + by < count]
    return lax.ppermute(value, axis, pairs)


def swapped(value, odd):
    count, groups = lax.axis_size("dom"), lax.axis_size("col")
    pairs = []
    for place in range(count):
        partner = place + 1 if (place % 2 == 1) == odd else place - 1
        for column in range(groups):
            if 0 <= partner < count:
                pairs.append((place * groups + column, partner * groups + column))
            else:
                beside = column ^ 1 if column ^ 1 < groups else column
                pairs.append((place * groups + column, place * groups + beside))
    return lax.ppermute(value, ("dom", "col"), pairs)


def left_half(shape):
    return lax.broadcasted_iota(jnp.int32, shape, len(shape) - 1) < PN


def split(value):
    high = value.astype(jnp.bfloat16)
    low = (value - high.astype(jnp.float32)).astype(jnp.bfloat16)
    return high, low


def tile(ref, index):
    return ref[:, index * LANES : (index + 1) * LANES]


def put(ref, index, value):
    ref[:, index * LANES : (index + 1) * LANES] = value


class Slots:
    def __init__(self, sources, targets, sems):
        self.local, self.partner = targets
        self.copies = [
            pltpu.make_async_copy(source, target, sems.at[place])
            for place, (source, target) in enumerate(zip(sources, targets))
        ]
        for copy in self.copies:
            copy.start()

    def wait(self):
        for copy in self.copies:
            copy.wait()


def live(count_ref, slot):
    return jnp.where(slot < count_ref[0], 1.0, 0.0)


def chunked(sources, targets, sems, chunk):
    copies = []
    for start in range(0, targets[0].shape[1], chunk):
        lanes = pl.ds(start, chunk)
        group = []
        for source, target in zip(sources, targets):
            group.append(
                pltpu.make_async_copy(source.at[:, lanes], target.at[:, lanes], sems.at[len(copies) * len(targets) + len(group)])
            )
        copies.append(group)
    return copies


def block_diagonal(high, low):
    mask = left_half((PN, LANES)).astype(jnp.bfloat16)
    other = (1 - left_half((PN, LANES)).astype(jnp.int32)).astype(jnp.bfloat16)
    return (
        jnp.concatenate([high * mask, high * other], axis=0),
        jnp.concatenate([low * mask, low * other], axis=0),
    )


def pair_product(rows, high, low):
    row_high, row_low = split(rows)
    product = jnp.dot(
        jnp.concatenate([row_high, row_low], axis=0),
        jnp.concatenate(block_diagonal(high, low), axis=1),
        preferred_element_type=jnp.float32,
    )
    count = rows.shape[0]
    return product[:count, :LANES] + (product[count:, :LANES] + product[:count, LANES:])


def fill_twins(field_tile, twin_ref, patch):
    swapped = pltpu.roll(field_tile, PN, 1)
    left = left_half(field_tile.shape)
    twin_ref[patch] = jnp.where(left, field_tile, swapped)
    twin_ref[patch + 1] = jnp.where(left, swapped, field_tile)


def side_by_side(first, second):
    return jnp.where(left_half(first.shape), first, second)


def scatter(force, step, targets):
    for slot in (2 * step, 2 * step + 1):
        for ref, patch, sign in targets(slot):
            ref[patch] = ref[patch] + force if sign > 0 else ref[patch] - force


def folded(total_ref, patch, other_ref):
    first = side_by_side(total_ref[patch], other_ref[patch])
    second = side_by_side(total_ref[patch + 1], other_ref[patch + 1])
    first = first + pltpu.roll(first, PN, 1)
    second = second + pltpu.roll(second, PN, 1)
    return jnp.where(left_half(first.shape), first, second)


def clear(total_ref):
    zero = jnp.zeros(total_ref.shape[1:], jnp.float32)
    for patch in range(total_ref.shape[0]):
        total_ref[patch] = zero


def prepare_kernel(
    field_hbm, stiff_hbm, contact_hbm, local_hbm, partner_hbm,
    field_ref, elastic_ref, stiff_high_ref, stiff_low_ref, contact_high_ref, contact_low_ref, local_ref, partner_ref,
    stiff_ref, contact_ref, sems, contact_sems, table_sems,
):
    chunk = stiff_ref.shape[1] // CHUNKS
    tiles = chunk // LANES
    copies = chunked((field_hbm, stiff_hbm), (field_ref, stiff_ref), sems, chunk)
    contact_copies = chunked((contact_hbm,), (contact_ref,), contact_sems, chunk)
    for group in copies + contact_copies:
        for copy in group:
            copy.start()
    slots = Slots((local_hbm, partner_hbm), (local_ref, partner_ref), table_sems)
    for place, group in enumerate(copies):
        for copy in group:
            copy.wait()
        for index in range(place * tiles, (place + 1) * tiles):
            high, low = split(tile(stiff_ref, index))
            put(stiff_high_ref, index, high)
            put(stiff_low_ref, index, low)
            put(elastic_ref, index, pair_product(tile(field_ref, index), high, low))
    for place, group in enumerate(contact_copies):
        for copy in group:
            copy.wait()
        for index in range(place * tiles, (place + 1) * tiles):
            high, low = split(tile(contact_ref, index))
            put(contact_high_ref, index, high)
            put(contact_low_ref, index, low)
    slots.wait()


def couple_kernel(
    count_ref, local_vmem, partner_vmem, field_ref, elastic_ref, halo_ref, high_ref, low_ref,
    total_ref, other_ref, gap_ref, force_ref, own_ref, spread_ref, even_ref, odd_ref,
    local_ref, partner_ref, table_sems, twin_ref,
):
    slots = Slots((local_vmem, partner_vmem), (local_ref, partner_ref), table_sems)
    patches = field_ref.shape[1] // PN
    clear(total_ref)
    clear(other_ref)
    for index in range(patches // 2):
        fill_twins(tile(field_ref, index), twin_ref, 2 * index)
    for index in range(NB // 2):
        fill_twins(tile(halo_ref, index), twin_ref, patches + 2 * index)
    slots.wait()

    def slot_gap(slot):
        return (twin_ref[slots.local[slot]] - twin_ref[slots.partner[slot]]) * live(count_ref, slot)

    def targets(slot):
        ref = (total_ref, other_ref)[slot % 2]
        return (ref, slots.local[slot], 1), (ref, slots.partner[slot], -1)

    for step in range(high_ref.shape[1] // LANES):
        gap = side_by_side(slot_gap(2 * step), slot_gap(2 * step + 1))
        force = pair_product(gap, tile(high_ref, step), tile(low_ref, step))
        put(gap_ref, step, gap)
        put(force_ref, step, force)
        scatter(force, step, targets)
    even = lax.axis_index("dom") % 2 == 0
    for index in range(NB // 2):
        value = tile(elastic_ref, index) + folded(total_ref, 2 * index, other_ref)
        spread = folded(total_ref, patches + 2 * index, other_ref)
        put(own_ref, index, value)
        put(spread_ref, index, spread)
        put(even_ref, index, jnp.where(even, spread, value))
        put(odd_ref, index, jnp.where(even, value, spread))


def by_column(product, columns):
    total = product[:columns]
    for part in range(1, product.shape[0] // columns):
        total = total + product[part * columns : (part + 1) * columns]
    return total


class Sums:
    def __init__(self, columns):
        self.columns = columns
        self.values = {}

    def add(self, place, product):
        product = by_column(product, self.columns)
        self.values[place] = self.values[place] + product if place in self.values else product

    def load(self, ref):
        for place in range(SUMS):
            self.values[place] = ref[place * self.columns : (place + 1) * self.columns]

    def store(self, ref):
        for place in range(SUMS):
            zero = jnp.zeros((self.columns, LANES), jnp.float32)
            ref[place * self.columns : (place + 1) * self.columns] = self.values.get(place, zero)


def weights_of(weight_ref, index, rows):
    parts = weight_ref.shape[0]
    return jnp.concatenate(
        [
            jnp.broadcast_to(weight_ref[part : part + 1, index * LANES : (index + 1) * LANES], (rows // parts, LANES))
            for part in range(parts)
        ],
        axis=0,
    )


def add_energy(sums, trial_rows, field_part, field_force, image_part, image_force):
    rest = field_part - trial_rows * image_part
    sums.add(5, rest * (field_force - trial_rows * image_force))
    sums.add(6, rest * image_force)
    sums.add(7, image_part * image_force)


def lift_kernel(
    local_vmem, partner_vmem, field_ref, total_ref, other_ref, field_elastic_ref, stiff_high_ref, stiff_low_ref, weight_ref,
    image_ref, elastic_ref, near_ref, sums_ref, trial_ref,
    local_ref, partner_ref, table_sems, twin_ref, *, columns,
):
    slots = Slots((local_vmem, partner_vmem), (local_ref, partner_ref), table_sems)
    rows = field_ref.shape[0]
    patches = field_ref.shape[1] // PN
    lead = NB // 2
    sums = Sums(columns)
    for index in range(patches // 2):
        field_tile = tile(field_ref, index)
        weight_tile = weights_of(weight_ref, index, rows)
        sums.add(0, field_tile * field_tile)
        sums.add(8, weight_tile * field_tile)
        if index < lead:
            continue
        image_tile = tile(field_elastic_ref, index) + folded(total_ref, 2 * index, other_ref)
        put(image_ref, index - lead, image_tile)
        fill_twins(image_tile, twin_ref, 2 * index)
        product = pair_product(image_tile, tile(stiff_high_ref, index), tile(stiff_low_ref, index))
        put(elastic_ref, index - lead, product)
        sums.add(1, field_tile * image_tile)
        sums.add(4, image_tile * image_tile)
        sums.add(9, weight_tile * image_tile)
    across = jnp.sum(sums.values[1], axis=1, keepdims=True)
    square = jnp.sum(sums.values[4], axis=1, keepdims=True)
    some = square > 0.0
    trial = jnp.where(some, across / jnp.where(some, square, 1.0), 0.0)
    trial = jnp.broadcast_to(trial, (columns, LANES))
    trial_ref[...] = trial
    trial_rows = jnp.concatenate([trial] * (rows // columns), axis=0)
    for index in range(lead, patches // 2):
        field_tile, image_tile = tile(field_ref, index), tile(image_ref, index - lead)
        rest = field_tile - trial_rows * image_tile
        sums.add(2, rest * rest)
        sums.add(3, rest * image_tile)
        add_energy(
            sums, trial_rows, field_tile, tile(field_elastic_ref, index), image_tile, tile(elastic_ref, index - lead)
        )
    sums.store(sums_ref)
    twin_ref[patches] = jnp.zeros(twin_ref.shape[1:], jnp.float32)
    slots.wait()

    def inner(patch):
        return twin_ref[jnp.where((patch >= NB) & (patch < patches), patch, patches)]

    def inner_gap(slot):
        return inner(slots.local[slot]) - inner(slots.partner[slot])

    for step in range(near_ref.shape[1] // LANES):
        put(near_ref, step, side_by_side(inner_gap(2 * step), inner_gap(2 * step + 1)))


def energy_kernel(
    count_ref, local_vmem, partner_vmem, field_ref, field_elastic_ref, gap_ref, force_ref, own_ref, spread_ref,
    even_ref, odd_ref, near_ref, stiff_high_ref, stiff_low_ref, contact_high_ref, contact_low_ref, weight_ref,
    sums_ref, trial_ref,
    lead_ref, lead_elastic_ref, image_force_ref, moment_ref,
    local_ref, partner_ref, table_sems, twin_ref, *, columns,
):
    slots = Slots((local_vmem, partner_vmem), (local_ref, partner_ref), table_sems)
    rows = field_ref.shape[0]
    patches = field_ref.shape[1] // PN
    lead = NB // 2
    place, last = lax.axis_index("dom"), lax.axis_size("dom") - 1
    even = place % 2 == 0
    trial = trial_ref[...]
    trial_rows = jnp.concatenate([trial] * (rows // columns), axis=0)
    sums = Sums(columns)
    sums.load(sums_ref)
    for index in range(lead):
        first, second = tile(even_ref, index), tile(odd_ref, index)
        received = jnp.where(place > 0, jnp.where(even, second, first), 0.0)
        far_tile = jnp.where(place < last, jnp.where(even, first, second) + tile(spread_ref, index), 0.0)
        fill_twins(far_tile, twin_ref, NB + 2 * index)
        field_tile = tile(field_ref, index)
        image_tile = tile(own_ref, index) + received
        put(lead_ref, index, image_tile)
        fill_twins(image_tile, twin_ref, 2 * index)
        product = pair_product(image_tile, tile(stiff_high_ref, index), tile(stiff_low_ref, index))
        put(lead_elastic_ref, index, product)
        rest = field_tile - trial_rows * image_tile
        sums.add(1, field_tile * image_tile)
        sums.add(2, rest * rest)
        sums.add(3, rest * image_tile)
        sums.add(4, image_tile * image_tile)
        sums.add(9, weights_of(weight_ref, index, rows) * image_tile)
        add_energy(sums, trial_rows, field_tile, tile(field_elastic_ref, index), image_tile, product)
    twin_ref[2 * NB] = jnp.zeros(twin_ref.shape[1:], jnp.float32)
    slots.wait()

    def outer(patch):
        far = patch >= patches
        return twin_ref[jnp.where(far, patch - patches + NB, jnp.where(patch < NB, patch, 2 * NB))]

    def outer_gap(slot):
        return outer(slots.local[slot]) - outer(slots.partner[slot])

    for step in range(contact_high_ref.shape[1] // LANES):
        gap = tile(near_ref, step) + side_by_side(outer_gap(2 * step), outer_gap(2 * step + 1))
        lives = [jnp.full(gap.shape, live(count_ref, 2 * step + side), jnp.float32) for side in range(2)]
        gap = gap * side_by_side(*lives)
        force = pair_product(gap, tile(contact_high_ref, step), tile(contact_low_ref, step))
        put(image_force_ref, step, force)
        add_energy(sums, trial_rows, tile(gap_ref, step), tile(force_ref, step), gap, force)
    lane = lax.broadcasted_iota(jnp.int32, (columns, LANES), 1)
    column = lax.broadcasted_iota(jnp.int32, (columns, LANES), 0)
    for half in range(2):
        spread_out = jnp.zeros((columns, LANES), jnp.float32)
        for number in range(half * 8, min(half * 8 + 8, SUMS + 1)):
            value = trial if number == SUMS else jnp.sum(sums.values[number], axis=1, keepdims=True)
            spread_out = jnp.where(lane == column + columns * (number % 8), value, spread_out)
        row = jnp.sum(spread_out, axis=0, keepdims=True)
        moment_ref[:, :, half * LANES : (half + 1) * LANES] = jnp.broadcast_to(
            row[None], (moment_ref.shape[0], 1, LANES)
        )


def settle_kernel(
    local_vmem, partner_vmem, force_ref, far_spread_ref, local_ref, partner_ref, table_sems, total_ref, other_ref, *, patches
):
    slots = Slots((local_vmem, partner_vmem), (local_ref, partner_ref), table_sems)
    clear(total_ref)
    clear(other_ref)
    slots.wait()

    def targets(slot):
        partner = slots.partner[slot]
        return (((total_ref, other_ref)[slot % 2], jnp.where(partner < patches, NB, partner - patches), -1),)

    for step in range(force_ref.shape[1] // LANES):
        scatter(tile(force_ref, step), step, targets)
    for index in range(NB // 2):
        put(far_spread_ref, index, folded(total_ref, 2 * index, other_ref))


def gather_kernel(
    local_vmem, partner_vmem, force_ref, lead_elastic_ref, elastic_ref, twice_ref,
    local_ref, partner_ref, table_sems, total_ref, other_ref,
):
    slots = Slots((local_vmem, partner_vmem), (local_ref, partner_ref), table_sems)
    patches = twice_ref.shape[1] // PN
    lead = NB // 2
    clear(total_ref)
    clear(other_ref)
    slots.wait()

    def targets(slot):
        partner = slots.partner[slot]
        ref = (total_ref, other_ref)[slot % 2]
        return (ref, slots.local[slot], 1), (ref, jnp.where(partner < patches, partner, patches), -1)

    for step in range(force_ref.shape[1] // LANES):
        scatter(tile(force_ref, step), step, targets)
    for index in range(patches // 2):
        product = tile(lead_elastic_ref, index) if index < lead else tile(elastic_ref, index - lead)
        put(twice_ref, index, product + folded(total_ref, 2 * index, other_ref))


def scale_kernel(moment_ref, scale_ref, gradient_ref, *, columns, groups):
    devices = moment_ref.shape[0]

    def moment(place):
        half = place // 8
        value = moment_ref[:, half * LANES : (half + 1) * LANES]
        shift = (LANES - columns * (place % 8)) % LANES
        if shift:
            value = pltpu.roll(value, shift, 1)
        return value.reshape(devices // 8, 8, LANES)

    def total(value):
        value = jnp.sum(value, axis=0)
        width = groups
        while width < 8:
            value = value + pltpu.roll(value, width, 0)
            width *= 2
        return value

    norm = total(moment(0))
    bend = total(moment(1))
    first_step = norm / bend
    change = first_step[None] - moment(SUMS)
    square = moment(4)
    mixed = moment(3)
    norm_next = total(moment(2) - 2.0 * change * mixed + change * change * square)
    drift = total(mixed - change * square)
    curve = total(moment(5) - 2.0 * change * moment(6) + change * change * moment(7))
    ratio = norm_next / norm
    bend_next = curve + 2.0 * ratio * drift + ratio * ratio * bend
    second_step = norm_next / bend_next
    on_field = first_step + second_step * (1.0 + ratio)
    on_image = -second_step * first_step
    gradient = on_field * total(moment(8)) + on_image * total(moment(9))
    gradient_ref[...] = gradient
    mine = lax.broadcasted_iota(jnp.int32, (8, LANES), 0) == lax.axis_index("col")
    diagonal = lax.broadcasted_iota(jnp.int32, (columns, LANES), 0) == lax.broadcasted_iota(
        jnp.int32, (columns, LANES), 1
    )
    for place, value in enumerate((on_field, on_image)):
        own = jnp.sum(jnp.where(mine, value, 0.0), axis=0, keepdims=True)
        own = jnp.sum(jnp.where(diagonal, own, 0.0), axis=1, keepdims=True)
        scale_ref[place * columns : (place + 1) * columns] = jnp.broadcast_to(own, (columns, LANES))


def own_step(gradient, columns, groups):
    lane = lax.broadcasted_iota(jnp.int32, (8, LANES), 1)
    row = lax.broadcasted_iota(jnp.int32, (8, LANES), 0)
    counted = jnp.where((lane < columns) & (row < groups), gradient * gradient, 0.0)
    square_total = jnp.sum(jnp.sum(counted, axis=1, keepdims=True), axis=0, keepdims=True)
    scaled = gradient / jnp.sqrt(square_total / (columns * groups) + 1e-06)
    return jnp.sum(jnp.where(row == lax.axis_index("col"), scaled, 0.0), axis=0, keepdims=True)[:, :columns]


def scale_rows(scale_ref, rows):
    columns = scale_ref.shape[0] // 2
    return (
        jnp.concatenate([scale_ref[:columns]] * (rows // columns), axis=0),
        jnp.concatenate([scale_ref[columns:]] * (rows // columns), axis=0),
    )


def last_kernel(
    scale_ref, gradient_ref, field_ref, image_ref, lead_ref, twice_ref, far_received_ref,
    solution_hbm, residual_hbm, step_hbm, solution_ref, residual_ref, step_ref, sems, step_sem, *, groups,
):
    field_rows, image_rows = scale_rows(scale_ref, field_ref.shape[0])
    chunk = field_ref.shape[1] // LAST_CHUNKS
    tiles = chunk // LANES
    copies = chunked((solution_ref, residual_ref), (solution_hbm, residual_hbm), sems, chunk)
    step_copy = pltpu.make_async_copy(step_ref, step_hbm, step_sem.at[0])
    for place, group in enumerate(copies):
        for index in range(place * tiles, (place + 1) * tiles):
            field_tile = tile(field_ref, index)
            image_tile = tile(lead_ref, index) if index < NB // 2 else tile(image_ref, index - NB // 2)
            twice_tile = tile(twice_ref, index)
            if index < NB // 2:
                twice_tile = twice_tile + tile(far_received_ref, index)
            put(solution_ref, index, field_rows * field_tile + image_rows * image_tile)
            put(residual_ref, index, field_tile - field_rows * image_tile - image_rows * twice_tile)
        for copy in group:
            copy.start()
        if place == 0:
            step_ref[...] = own_step(gradient_ref[...], scale_ref.shape[0] // 2, groups)
            step_copy.start()
    step_copy.wait()
    for group in copies:
        for copy in group:
            copy.wait()


def shards(right_side, stiffness, contact, pair_local, pair_partner, pair_count, objective_weight):
    components, columns, nodes = right_side.shape
    rows = components * columns
    patches = nodes // PN
    groups = lax.axis_size("col")
    chain_length = lax.axis_size("dom")
    devices = chain_length * groups
    f32 = jnp.float32
    width = NB * PN
    call = functools.partial(
        pl.pallas_call, compiler_params=pltpu.CompilerParams(vmem_limit_bytes=8 * 1024 * 1024)
    )
    shape = jax.ShapeDtypeStruct
    wide = shape((rows, nodes), f32)
    narrow = shape((rows, width), f32)
    parts = [shape(block.shape, jnp.bfloat16) for block in (stiffness, stiffness, contact, contact)]

    def in_hbm(value):
        return pltpu.with_memory_space_constraint(value, pltpu.HBM)

    field_hbm = in_hbm(right_side.reshape(rows, nodes))
    pairs = (in_hbm(pair_local), in_hbm(pair_partner))
    slots = shape((rows, contact.shape[1]), f32)

    def scratch(count, copies=1):
        return [
            pltpu.SMEM(pair_local.shape, jnp.int32),
            pltpu.SMEM(pair_partner.shape, jnp.int32),
            pltpu.SemaphoreType.DMA((2,)),
        ] + [pltpu.VMEM((count, rows, LANES), f32)] * copies

    halo = shifted(right_side[:, :, :width], "dom", -1).reshape(rows, width)
    field, field_elastic, stiff_high, stiff_low, contact_high, contact_low, *tables = call(
        prepare_kernel,
        out_shape=(wide, wide, *parts, *(shape(pair.shape, jnp.int32) for pair in pairs)),
        in_specs=[HBM] * 5,
        out_specs=(VMEM,) * 8,
        scratch_shapes=[
            pltpu.VMEM(stiffness.shape, f32),
            pltpu.VMEM(contact.shape, f32),
            pltpu.SemaphoreType.DMA((2 * CHUNKS,)),
            pltpu.SemaphoreType.DMA((CHUNKS,)),
            pltpu.SemaphoreType.DMA((2,)),
        ],
        name="prepare",
    )(field_hbm, in_hbm(stiffness), in_hbm(contact), *pairs)
    total, other, gap, force, own, spread, even, odd = call(
        couple_kernel,
        out_shape=(*[shape((patches + NB, rows, LANES), f32)] * 2, slots, slots, narrow, narrow, narrow, narrow),
        in_specs=[SMEM] + [VMEM] * 7,
        out_specs=(VMEM,) * 8,
        scratch_shapes=scratch(patches + NB),
        name="couple",
    )(pair_count, *tables, field, field_elastic, halo, contact_high, contact_low)
    even = swapped(even, False)
    odd = swapped(odd, True)
    tail = shape((rows, nodes - width), f32)
    image, elastic, near, sums, trial = call(
        functools.partial(lift_kernel, columns=columns),
        out_shape=(tail, tail, slots, shape((SUMS * columns, LANES), f32), shape((columns, LANES), f32)),
        in_specs=[VMEM] * 9,
        out_specs=(VMEM,) * 5,
        scratch_shapes=scratch(patches + 1),
        name="lift",
    )(*tables, field, total, other, field_elastic, stiff_high, stiff_low, objective_weight)
    lead, lead_elastic, image_force, moments = call(
        functools.partial(energy_kernel, columns=columns),
        out_shape=(narrow, narrow, slots, shape((devices, 1, MOMENT_LANES), f32)),
        in_specs=[SMEM] + [VMEM] * 18,
        out_specs=(VMEM,) * 4,
        scratch_shapes=scratch(2 * NB + 1),
        name="energy",
    )(
        pair_count, *tables, field, field_elastic, gap, force, own, spread, even, odd, near,
        stiff_high, stiff_low, contact_high, contact_low, objective_weight, sums, trial,
    )
    gathered = lax.all_to_all(moments, ("dom", "col"), 0, 0, tiled=True).reshape(devices, MOMENT_LANES)
    far_spread = call(
        functools.partial(settle_kernel, patches=patches),
        out_shape=narrow,
        in_specs=[VMEM] * 3,
        out_specs=VMEM,
        scratch_shapes=scratch(NB + 1, 2),
        cost_estimate=pl.CostEstimate(flops=10**9, bytes_accessed=rows * nodes * 4, transcendentals=0),
        name="settle",
    )(*tables, image_force)
    far_received = shifted(far_spread, "dom", 1)
    twice = call(
        gather_kernel,
        out_shape=wide,
        in_specs=[VMEM] * 5,
        out_specs=VMEM,
        scratch_shapes=scratch(patches + 1, 2),
        cost_estimate=pl.CostEstimate(flops=10**9, bytes_accessed=3 * rows * nodes * 4, transcendentals=0),
        name="gather",
    )(*tables, image_force, lead_elastic, elastic)
    scales, gradient = call(
        functools.partial(scale_kernel, columns=columns, groups=groups),
        out_shape=(shape((2 * columns, LANES), f32), shape((8, LANES), f32)),
        in_specs=[VMEM],
        out_specs=(VMEM,) * 2,
        cost_estimate=pl.CostEstimate(flops=10**9, bytes_accessed=devices * MOMENT_LANES * 4, transcendentals=0),
        name="scale",
    )(gathered)
    solution_field, residual, step = call(
        functools.partial(last_kernel, groups=groups),
        out_shape=(wide, wide, shape((1, columns), f32)),
        in_specs=[VMEM] * 7,
        out_specs=(HBM,) * 3,
        scratch_shapes=[pltpu.VMEM((rows, nodes), f32)] * 2
        + [
            pltpu.VMEM((1, columns), f32),
            pltpu.SemaphoreType.DMA((2 * LAST_CHUNKS,)),
            pltpu.SemaphoreType.DMA((1,)),
        ],
        name="last",
    )(scales, gradient, field, image, lead, twice, far_received)
    return (
        solution_field.reshape(right_side.shape),
        residual.reshape(right_side.shape),
        step.reshape(columns),
    )


def solution(mesh):
    placed = (
        P(None, "col", "dom"),
        P(None, "dom"),
        P(None, "dom"),
        P("dom"),
        P("dom"),
        P("dom"),
        P(None, "dom"),
    )
    return jax.shard_map(
        shards,
        mesh=mesh,
        in_specs=placed,
        out_specs=(P(None, "col", "dom"), P(None, "col", "dom"), P("col")),
        check_vma=False,
    )
```
